32 devices in a mesh: dp: 8 (over z, core), frames: 4 (over y, x).
Axes of the slice: x: 2, y: 2, z: 4, core: 2. Of those that a mesh axis runs over, the one named last changes fastest.
Arguments:
- latents: bfloat16 [8, 8, 2, 32, 640], P('dp', 'frames'), may hold values from -6 to 6
- lengths: int32 [8, 4], P('dp', 'frames'), may hold values from 1 to 2
- norm_gain: float32 [640], replicated, may hold values from 0.1 to 1.9
- norm_bias: float32 [640], replicated, may hold values from -3 to 3
- spatial_weight: bfloat16 [5760, 640], P('dp'), may hold values from -0.078125 to 0.078125
- temporal_weight: bfloat16 [1920, 640], P('dp'), may hold values from -0.125 to 0.125
- cotangent: bfloat16 [8, 8, 2, 32, 640], P('dp', 'frames'), may hold values from -6 to 6
Outputs:
- output: bfloat16 [8, 8, 2, 32, 640], P('dp', 'frames')
- input_grad: bfloat16 [8, 8, 2, 32, 640], P('dp', 'frames')
The draws below stay inside these ranges and needn't reach their ends.
Inputs may be any that keep to these rules, and one draw needn't show every extreme that they name: A device's first lengths slots hold frames of its clip, in order; the other slots are padding.
All inputs are finite; a program needn't handle non-finite values.
Results may differ from the reference program's by a relative error of at most 0.0039.
Values may be sent and summed in bfloat16 or wider, within the bound.
A program may use at most 64 MiB of HBM per device.

```python
import jax
import jax.numpy as jnp
from jax import lax

CH = 640
GROUPS = 32
FCAP = 2
HH = 2
WW = 32
PIX = 64
NFR = 8
CLIPS = 8
N_FRAMES = 4


def place_ends(drawn, rng, smallest, largest):
    longest = drawn.shape.index(max(drawn.shape))
    spots = []
    for shift in (0, 1):
        where = [jax.random.randint(jax.random.fold_in(rng, axis), (), 0, length) for axis, length in enumerate(drawn.shape)]
        where[longest] = (where[longest] + shift) % drawn.shape[longest]
        spots.append(tuple(where))
    return drawn.at[spots[0]].set(smallest).at[spots[1]].set(largest)


def levels(own_key, dims, cuts, least, largest):
    level = 1.0
    for axis_at, shards_of in cuts:
        heights = jax.random.uniform(jax.random.fold_in(jax.random.fold_in(own_key, 6), axis_at), (shards_of,), jnp.float32, least / len(cuts), largest / len(cuts))
        level = level * jnp.repeat(jnp.exp(heights), dims[axis_at] // shards_of).reshape((-1,) + (1,) * (len(dims) - 1 - axis_at))
    return level


def gaussian(stream_key, extent, scale, bound, cuts=(), kind=jnp.bfloat16):
    values = scale * jax.random.normal(stream_key, extent, jnp.float32)
    if cuts:
        values = values * levels(stream_key, extent, cuts, -0.22, 0.18)
    return jnp.clip(values, -bound, bound).astype(kind)


def setup_inputs(seed: int = 0) -> dict:
    arg_keys = jax.random.split(jax.random.key(seed), 8)
    return {
        "latents": gaussian(arg_keys[0], (CLIPS, NFR, HH, WW, CH), 1.0, 6.0, ((0, 8), (1, 4))),
        "lengths": place_ends(jax.random.randint(arg_keys[1], (CLIPS, N_FRAMES), 1, FCAP + 1), jax.random.fold_in(arg_keys[1], 1), 1, FCAP).astype(jnp.int32),
        "norm_gain": jnp.clip(1.0 + 0.18 * jax.random.normal(arg_keys[2], (CH,), jnp.float32), 0.1, 1.9),
        "norm_bias": gaussian(arg_keys[3], (CH,), 0.5, 3.0, (), jnp.float32),
        "spatial_weight": gaussian(arg_keys[4], (9 * CH, CH), (9 * CH) ** -0.5, 0.078125, ((0, 8),)),
        "temporal_weight": gaussian(arg_keys[5], (3 * CH, CH), (3 * CH) ** -0.5, 0.125, ((0, 8),)),
        "cotangent": gaussian(arg_keys[6], (CLIPS, NFR, HH, WW, CH), 1.0, 6.0, ((0, 8), (1, 4))),
    }


epsilon = 1e-05

def normalize(frames_in, norm_gain, norm_bias):
    shaped = frames_in.reshape(frames_in.shape[0], -1, GROUPS, CH // GROUPS)
    centre = lax.optimization_barrier(jnp.mean(shaped, axis=(1, 3), keepdims=True))
    spread = lax.optimization_barrier(jnp.mean(jnp.square(shaped - centre), axis=(1, 3), keepdims=True))
    inverse = lax.rsqrt(spread + epsilon)
    scaled = (shaped - centre) * inverse
    shifted = scaled.reshape(frames_in.shape) * norm_gain + norm_bias
    return (scaled, inverse, shifted)

def norm_backward(active_grad, scaled, inverse, shifted, norm_gain):
    sigma = jax.nn.sigmoid(shifted)
    shift_grad = active_grad * sigma * (1.0 + shifted * (1.0 - sigma))
    norm_grad = (shift_grad * norm_gain).reshape(scaled.shape)
    first = lax.optimization_barrier(jnp.mean(norm_grad, axis=(1, 3), keepdims=True))
    second = lax.optimization_barrier(jnp.mean(norm_grad * scaled, axis=(1, 3), keepdims=True))
    return (inverse * (norm_grad - first - scaled * second)).reshape(active_grad.shape)

def patchify(active):
    padded = jnp.pad(active, ((0, 0), (1, 1), (1, 1), (0, 0)))
    pieces = [padded[:, row:row + HH, col:col + WW, :] for row in range(3) for col in range(3)]
    return jnp.concatenate(pieces, axis=-1).reshape(-1, 9 * CH)

def unpatchify(patch_grad):
    count = patch_grad.shape[0] // (HH * WW)
    shaped = patch_grad.reshape(count, HH, WW, 9, CH)
    total = jnp.zeros((count, HH + 2, WW + 2, CH), jnp.float32)
    for row in range(3):
        for col in range(3):
            total = total + jnp.pad(shaped[:, :, :, row * 3 + col, :], ((0, 0), (row, 2 - row), (col, 2 - col), (0, 0)))
    return total[:, 1:-1, 1:-1, :]

def contract_rows(left, right):
    return lax.dot_general(left, right, (((1,), (1,)), ((), ())), preferred_element_type=jnp.float32)

def reference(latents, lengths, norm_gain, norm_bias, spatial_weight, temporal_weight, cotangent):
    index = jnp.arange(NFR, dtype=jnp.int32)
    owner = index // FCAP
    place = index % FCAP
    first_w = temporal_weight[:CH]
    centre_w = temporal_weight[CH:2 * CH]
    last_w = temporal_weight[2 * CH:]

    def one_clip(packed):
        clip_in, clip_cot, length_row = packed
        valid = place < length_row[owner]
        marked = jnp.where(valid, index, jnp.int32(-1))
        before = jnp.concatenate([jnp.full((1,), -1, jnp.int32), lax.cummax(marked, axis=0)[:-1]])
        previous = jnp.where(before < 0, jnp.int32(NFR), before).astype(jnp.int32)
        later = jnp.where(valid, index, jnp.int32(NFR))
        following = jnp.concatenate([lax.cummin(later, axis=0, reverse=True)[1:], jnp.full((1,), NFR, jnp.int32)]).astype(jnp.int32)
        keep = valid[:, None, None, None]
        values = clip_in.astype(jnp.float32)
        scaled, inverse, shifted = normalize(values, norm_gain, norm_bias)
        active = jax.nn.silu(shifted).astype(jnp.bfloat16)
        spatial = jnp.dot(patchify(active), spatial_weight, preferred_element_type=jnp.float32).astype(jnp.bfloat16)
        spatial = spatial.reshape(NFR, PIX, CH)
        extended = jnp.concatenate([spatial, jnp.zeros((1, PIX, CH), jnp.bfloat16)])
        temporal = jnp.dot(extended[previous].reshape(-1, CH), first_w, preferred_element_type=jnp.float32)
        temporal = temporal + jnp.dot(spatial.reshape(-1, CH), centre_w, preferred_element_type=jnp.float32)
        temporal = temporal + jnp.dot(extended[following].reshape(-1, CH), last_w, preferred_element_type=jnp.float32)
        temporal = temporal.reshape(NFR, HH, WW, CH)
        output = jnp.where(keep, values + temporal, 0.0).astype(jnp.bfloat16)
        upstream = jnp.where(keep, clip_cot, jnp.zeros_like(clip_cot)).reshape(NFR, PIX, CH)
        grown = jnp.concatenate([upstream, jnp.zeros((1, PIX, CH), jnp.bfloat16)])
        spatial_grad = contract_rows(upstream.reshape(-1, CH), centre_w)
        spatial_grad = spatial_grad + contract_rows(grown[following].reshape(-1, CH), first_w)
        spatial_grad = spatial_grad + contract_rows(grown[previous].reshape(-1, CH), last_w)
        spatial_grad = spatial_grad.astype(jnp.bfloat16)
        active_grad = unpatchify(contract_rows(spatial_grad, spatial_weight))
        latent_grad = norm_backward(active_grad, scaled, inverse, shifted, norm_gain)
        input_grad = jnp.where(keep, clip_cot.astype(jnp.float32) + latent_grad, 0.0).astype(jnp.bfloat16)
        return (output, input_grad)
    return lax.map(one_clip, (latents, cotangent, lengths))
```

```python
import functools

import jax
import jax.numpy as jnp
from jax import lax
from jax.experimental import pallas as pl
from jax.experimental.pallas import tpu as pltpu
from jax.sharding import PartitionSpec as P

CH = 640
GROUPS = 32
HH = 2
WW = 32
PIX = 64


epsilon = 1e-05


def padded_2(cells, sides, width):
    for axis, dim in sides:
        count = lax.axis_size(axis)
        ends = count - 1
        head = lax.slice_in_dim(cells, 0, width, axis=dim)
        tail = lax.slice_in_dim(cells, cells.shape[dim] - width, cells.shape[dim], axis=dim)
        cells = jnp.concatenate(
            [
                lax.ppermute(tail, axis, [(i, (i + 1) % count) for i in range(ends)]),
                cells,
                lax.ppermute(head, axis, [((i + 1) % count, i) for i in range(ends)]),
            ],
            axis=dim,
        )
    return cells


def normalize(frames_in, norm_gain, norm_bias):
    shaped = frames_in.reshape(frames_in.shape[0], -1, GROUPS, CH // GROUPS)
    centre = jnp.mean(shaped, axis=(1, 3), keepdims=True)
    spread = jnp.mean(jnp.square(shaped - centre), axis=(1, 3), keepdims=True)
    inverse = lax.rsqrt(spread + epsilon)
    scaled = (shaped - centre) * inverse
    shifted = scaled.reshape(frames_in.shape) * norm_gain + norm_bias
    return (scaled, inverse, shifted)


def norm_backward(active_grad, scaled, inverse, shifted, norm_gain):
    sigma = jax.nn.sigmoid(shifted)
    shift_grad = active_grad * sigma * (1.0 + shifted * (1.0 - sigma))
    norm_grad = (shift_grad * norm_gain).reshape(scaled.shape)
    first = jnp.mean(norm_grad, axis=(1, 3), keepdims=True)
    second = jnp.mean(norm_grad * scaled, axis=(1, 3), keepdims=True)
    return (inverse * (norm_grad - first - scaled * second)).reshape(active_grad.shape)


def patchify(active):
    padded = jnp.pad(active, ((0, 0), (1, 1), (1, 1), (0, 0)))
    pieces = [padded[:, row : row + HH, col : col + WW, :] for row in range(3) for col in range(3)]
    return jnp.concatenate(pieces, axis=-1).reshape(-1, 9 * CH)


def unpatchify(patch_grad):
    count = patch_grad.shape[0] // (HH * WW)
    shaped = patch_grad.reshape(count, HH, WW, 9, CH)
    total = jnp.zeros((count, HH + 2, WW + 2, CH), jnp.float32)
    for row in range(3):
        for col in range(3):
            total = total + jnp.pad(
                shaped[:, :, :, row * 3 + col, :], ((0, 0), (row, 2 - row), (col, 2 - col), (0, 0))
            )
    return total[:, 1:-1, 1:-1, :]


def contract_rows(left, right):
    return lax.dot_general(
        left, right, (((1,), (1,)), ((), ())), preferred_element_type=jnp.float32
    )


def neighbours(frames_bf, count):
    last_frame = lax.dynamic_index_in_dim(frames_bf, count - 1, 0, keepdims=False)
    boundary = jnp.stack([frames_bf[0], last_frame])
    padded = padded_2(boundary, (("frames", 0),), 1)
    before_frames = jnp.concatenate([padded[0:1], frames_bf[:-1]])
    candidate = jnp.concatenate([frames_bf[1:], padded[3:4]])
    places = jnp.arange(frames_bf.shape[0], dtype=jnp.int32)
    after_frames = jnp.where((places + 1 < count)[:, None, None], candidate, padded[3:4])
    return (before_frames, after_frames)


def shards(latents, lengths, norm_gain, norm_bias, spatial_weight, temporal_weight, cotangent):
    clip_in = latents[0]
    clip_cot = cotangent[0]
    slots_here = clip_in.shape[0]
    count = lengths[0, 0]
    valid = jnp.arange(slots_here, dtype=jnp.int32) < count
    keep = valid[:, None, None, None]
    spatial_full, temporal_full = (
        lax.all_gather(spatial_weight, "dp", axis=0, tiled=True),
        lax.all_gather(temporal_weight, "dp", axis=0, tiled=True),
    )
    first_w = temporal_full[:CH]
    centre_w = temporal_full[CH : 2 * CH]
    last_w = temporal_full[2 * CH :]
    values = clip_in.astype(jnp.float32)
    scaled, inverse, shifted = normalize(values, norm_gain, norm_bias)
    active = jax.nn.silu(shifted).astype(jnp.bfloat16)
    patches = patchify(active)
    spatial = jnp.dot(patches, spatial_full, preferred_element_type=jnp.float32)
    spatial = spatial.astype(jnp.bfloat16).reshape(slots_here, PIX, CH)
    earlier, later_frames = neighbours(spatial, count)
    temporal = jnp.dot(earlier.reshape(-1, CH), first_w, preferred_element_type=jnp.float32)
    temporal = temporal + jnp.dot(
        spatial.reshape(-1, CH), centre_w, preferred_element_type=jnp.float32
    )
    temporal = temporal + jnp.dot(
        later_frames.reshape(-1, CH), last_w, preferred_element_type=jnp.float32
    )
    temporal = temporal.reshape(slots_here, HH, WW, CH)
    output = jnp.where(keep, values + temporal, 0.0).astype(jnp.bfloat16)
    upstream = jnp.where(keep, clip_cot, jnp.zeros_like(clip_cot)).reshape(slots_here, PIX, CH)
    up_before, up_after = neighbours(upstream, count)
    spatial_grad = contract_rows(upstream.reshape(-1, CH), centre_w)
    spatial_grad = spatial_grad + contract_rows(up_after.reshape(-1, CH), first_w)
    spatial_grad = spatial_grad + contract_rows(up_before.reshape(-1, CH), last_w)
    spatial_grad = spatial_grad.astype(jnp.bfloat16)
    patch_grad = contract_rows(spatial_grad, spatial_full)
    active_grad = unpatchify(patch_grad)
    latent_grad = norm_backward(active_grad, scaled, inverse, shifted, norm_gain)
    input_grad = jnp.where(keep, clip_cot.astype(jnp.float32) + latent_grad, 0.0).astype(
        jnp.bfloat16
    )
    return (output[None], input_grad[None])

MESH = pl.DeviceIdType.MESH
BLK = 80
PLANES = 4
TROWS = 3 * CH
CHUNK = 1536
STRIDE = 1408
EVENTS = ((1, 0), (2, 0), (3, 0), (2, 1), (2, 2), (3, 1), (3, 2), (1, 1))
DIRECT = (1, 2)
N_EV = len(EVENTS)
NT = (((1,), (1,)), ((), ()))


def row_of(plane, core, block):
    late = (block + 9) // 12
    early_row = (2 * plane + core) * 240 + block * BLK
    late_row = TROWS + plane * (CHUNK + 32) + core * 720 + (block - 3) * BLK
    return pl.multiple_of((1 - late) * early_row + late * late_row, 16)


def split3(rows):
    high = rows.astype(jnp.bfloat16)
    rest = rows - high.astype(jnp.float32)
    mid = rest.astype(jnp.bfloat16)
    low = (rest - mid.astype(jnp.float32)).astype(jnp.bfloat16)
    return high, mid, low


def dot32(left, right):
    return jnp.dot(left, right, preferred_element_type=jnp.float32)


def group_means(rows, gather_m, spread_m, size):
    high, mid, low = split3(rows)
    sums = dot32(high, gather_m) + dot32(mid, gather_m) + dot32(low, gather_m)
    high, mid, low = split3(sums * (1.0 / size))
    return dot32(high, spread_m) + dot32(mid, spread_m) + dot32(low, spread_m)


def frame_sums(cells):
    top = jnp.sum(cells[:PIX], axis=0, keepdims=True)
    low = jnp.sum(cells[PIX:], axis=0, keepdims=True)
    return top, low


def stack8(rows):
    return jnp.concatenate(list(rows) + [jnp.zeros((8 - len(rows), CH), jnp.float32)], axis=0)


def on_cells(top, low):
    return jnp.concatenate(
        [jnp.broadcast_to(top, (PIX, CH)), jnp.broadcast_to(low, (PIX, CH))], axis=0
    )


def kernel(
    len_hbm, lat_hbm, cot_hbm, gain_hbm, bias_hbm, ws_ref, wt_ref,
    out_ref, ig_ref,
    len_ref, lat_ref, cot_ref, gain_ref, bias_ref, in_sem, wbuf, patches, patch_grad, acc, sgrad, scaled_s, shifted_s, inv_s, spat, edge_up, edge_sp, halo_up, halo_sp,
    own_sem, sent, zr, xr, yr, rr, pr, orr, hs, hr,
):
    me = lax.axis_index("dp")
    fr = lax.axis_index("frames")
    plane = me // 2
    core = me % 2
    other = me + 1 - 2 * core
    fx = fr + 1 - 2 * (fr % 2)
    fy = (fr + 2) % 4
    fd = 3 - fr
    right = (fr + 1) % 4
    left = (fr + 3) % 4

    def plane_of(k):
        return (plane + 1 - 2 * (plane % 2), (plane + 2) % 4, 3 - plane)[k - 1]

    barrier = pltpu.get_barrier_semaphore()
    for k in (1, 2, 3):
        pl.semaphore_signal(barrier, inc=1, device_id=(2 * plane_of(k) + core, fr), device_id_type=MESH)
    for f in (fx, fy, fd):
        pl.semaphore_signal(barrier, inc=1, device_id=(me, f), device_id_type=MESH)
    pl.semaphore_signal(barrier, inc=1, device_id=(other, fr), device_id_type=MESH)

    own_t = pl.multiple_of(me * 240, 16)
    own_s = pl.multiple_of(TROWS + plane * (CHUNK + 32) + core * 720, 16)
    inputs = [
        pltpu.make_async_copy(src, dst, in_sem.at[n])
        for n, (src, dst) in enumerate(
            ((len_hbm, len_ref), (cot_hbm, cot_ref), (lat_hbm, lat_ref), (gain_hbm, gain_ref), (bias_hbm, bias_ref))
        )
    ]
    for copy in inputs:
        copy.start()
    local_t = pltpu.make_async_copy(wt_ref, wbuf.at[pl.ds(own_t, 240)], own_sem.at[0])
    local_s = pltpu.make_async_copy(ws_ref, wbuf.at[pl.ds(own_s, 720)], own_sem.at[1])
    local_t.start()
    local_s.start()

    for p in range(PLANES):
        base = TROWS + p * CHUNK
        if p > 0:
            wbuf[base : base + 32 * p, :] = jnp.zeros((32 * p, CH), jnp.bfloat16)
        if p < 3:
            wbuf[base + 1440 + 32 * p : base + CHUNK, :] = jnp.zeros((96 - 32 * p, CH), jnp.bfloat16)

    inputs[0].wait()
    inputs[1].wait()
    two = len_ref[0, 0] > 1
    cot_bf = cot_ref[...]
    edge_up[0] = cot_bf[:PIX]
    edge_up[1] = jnp.where(two, cot_bf[PIX:], cot_bf[:PIX])

    pl.semaphore_wait(barrier, 7)

    sent_rows = [0, 0, 0, 0]

    def send(src, row, count, lane, recv_sem, device):
        view = wbuf.at[pl.ds(row, count)]
        pltpu.make_async_remote_copy(
            src_ref=view if src is None else src, dst_ref=view, send_sem=sent.at[lane], recv_sem=recv_sem,
            device_id=device, device_id_type=MESH,
        ).start()
        sent_rows[lane] += count

    def arrived(count, recv_sem):
        view = wbuf.at[pl.ds(0, count)]
        pltpu.make_async_remote_copy(
            src_ref=view, dst_ref=view, send_sem=sent.at[0], recv_sem=recv_sem,
            device_id=(other, fr), device_id_type=MESH,
        ).wait_recv()

    def halo(edge, dest, k):
        copies = []
        for side, device in ((0, left), (1, right)):
            copy = pltpu.make_async_remote_copy(
                src_ref=edge.at[side], dst_ref=dest.at[side], send_sem=hs.at[k + side],
                recv_sem=hr.at[k + side], device_id=(me, device), device_id_type=MESH,
            )
            copy.start()
            copies.append(copy)
        return copies

    def z_send(k, block, recv_sem):
        rows = pl.ds(pl.multiple_of((block - 3) * BLK, 16), BLK)
        device = (2 * plane_of(k) + core, fr)
        send(ws_ref.at[rows], row_of(plane, core, block), BLK, 0, recv_sem, device)

    def z_first(k, recv_sem):
        device = (2 * plane_of(k) + core, fr)
        view = wbuf.at[pl.ds(row_of(plane, core, fr), BLK)]
        sent_rows[0] += BLK

        def go(src):
            pltpu.make_async_remote_copy(
                src_ref=src, dst_ref=view, send_sem=sent.at[0], recv_sem=recv_sem,
                device_id=device, device_id_type=MESH,
            ).start()

        @pl.when(fr < 3)
        def _():
            go(wt_ref.at[pl.ds(pl.multiple_of((fr % 3) * BLK, 16), BLK)])

        @pl.when(fr == 3)
        def _():
            go(ws_ref.at[pl.ds(0, BLK)])

    for e, (k, j) in enumerate(EVENTS):
        if j == 0:
            z_first(k, zr.at[e])
        else:
            z_send(k, 4 * j + fr, zr.at[e])
    send(wt_ref, own_t, 240, 3, orr.at[0], (other, fr))
    send(ws_ref, own_s, 720, 3, orr.at[1], (other, fr))
    up_copies = halo(edge_up, halo_up, 0)

    def send_direct():
        for f in range(4):
            z_send(DIRECT[0], 4 * DIRECT[1] + f, zr.at[N_EV + f])

    def to_core(row, k, j):
        send(None, row, BLK, 3, pr.at[3 * (k - 1) + j], (other, fr))

    def take_direct(f):
        k, j = DIRECT
        arrived(BLK, zr.at[N_EV + f])
        to_core(row_of(plane_of(k), core, 4 * j + f), k, j)

    def z(e):
        k, j = EVENTS[e]
        row = row_of(plane_of(k), core, 4 * j + fr)
        arrived(BLK, zr.at[e])
        send(None, row, BLK, 1, xr.at[e], (me, fx))
        send(None, row, BLK, 2, yr.at[e], (me, fy))
        to_core(row, k, j)

    def x(e):
        k, j = EVENTS[e]
        row = row_of(plane_of(k), core, 4 * j + fx)
        arrived(BLK, xr.at[e])
        if e % 2 == 0:
            send(None, row, BLK, 2, rr.at[e], (me, fy))
        to_core(row, k, j)

    def y(e):
        k, j = EVENTS[e]
        row = row_of(plane_of(k), core, 4 * j + fy)
        arrived(BLK, yr.at[e])
        if e % 2 == 1:
            send(None, row, BLK, 1, rr.at[e], (me, fx))
        to_core(row, k, j)

    def r(e):
        k, j = EVENTS[e]
        arrived(BLK, rr.at[e])
        to_core(row_of(plane_of(k), core, 4 * j + fd), k, j)

    def from_core(k, j):
        arrived(4 * BLK, pr.at[3 * (k - 1) + j])

    def chunk_rows(p):
        return pl.ds(pl.multiple_of(TROWS + p * CHUNK, 128), CHUNK)

    def chunk_lanes(p):
        return pl.ds(pl.multiple_of(p * STRIDE, 128), CHUNK)

    def forward(p):
        acc[...] += dot32(patches[:, chunk_lanes(p)], wbuf[chunk_rows(p), :])

    def backward(p):
        grad = lax.dot_general(
            sgrad[...], wbuf[chunk_rows(p), :], NT, preferred_element_type=jnp.float32
        )
        patch_grad[:, chunk_lanes(p)] += grad

    channel = lax.broadcasted_iota(jnp.int32, (CH, 128), 0)
    group = lax.broadcasted_iota(jnp.int32, (CH, 128), 1) * (CH // GROUPS)
    gather_m = ((channel >= group) & (channel < group + CH // GROUPS)).astype(jnp.float32).astype(jnp.bfloat16)
    channel = lax.broadcasted_iota(jnp.int32, (128, CH), 1)
    group = lax.broadcasted_iota(jnp.int32, (128, CH), 0) * (CH // GROUPS)
    spread_m = ((channel >= group) & (channel < group + CH // GROUPS)).astype(jnp.float32).astype(jnp.bfloat16)
    size = PIX * (CH // GROUPS)

    cell = lax.broadcasted_iota(jnp.int32, (2 * PIX, CH), 0)
    column = cell % WW

    def normalise():
        for copy in inputs[2:]:
            copy.wait()
        values = lat_ref[...].astype(jnp.float32)
        centre = group_means(stack8(frame_sums(values)), gather_m, spread_m, size)
        centred = values - on_cells(centre[0:1], centre[1:2])
        spread = group_means(stack8(frame_sums(centred * centred)), gather_m, spread_m, size)
        inverse = lax.rsqrt(spread + epsilon)
        inv_s[...] = inverse
        scaled = centred * on_cells(inverse[0:1], inverse[1:2])
        scaled_s[...] = scaled
        shifted_s[...] = scaled * gain_ref[...].reshape(1, CH) + bias_ref[...].reshape(1, CH)

    def make_patches():
        shifted = shifted_s[...]
        active = (shifted * jax.nn.sigmoid(shifted)).astype(jnp.bfloat16).astype(jnp.float32)
        zero = jnp.zeros((WW, CH), jnp.bfloat16)
        for dx in range(3):
            if dx == 1:
                moved = active
            elif dx == 0:
                moved = jnp.where(column == 0, 0.0, pltpu.roll(active, 1, 0))
            else:
                moved = jnp.where(column == WW - 1, 0.0, pltpu.roll(active, 2 * PIX - 1, 0))
            moved = moved.astype(jnp.bfloat16)
            quarters = [moved[q * WW : (q + 1) * WW] for q in range(4)]
            for dy in range(3):
                lanes = slice((3 * dy + dx) * CH, (3 * dy + dx + 1) * CH)
                if dy == 0:
                    rows = [zero, quarters[0], zero, quarters[2]]
                elif dy == 1:
                    rows = quarters
                else:
                    rows = [quarters[1], zero, quarters[3], zero]
                for q in range(4):
                    patches[q * WW : (q + 1) * WW, lanes] = rows[q]

    def spatial_gradient():
        for copy in up_copies:
            copy.wait()
        first, second = cot_bf[:PIX], cot_bf[PIX:]
        none = jnp.zeros((PIX, CH), jnp.bfloat16)
        second = jnp.where(two, second, none)
        after_edge = jnp.where(fr < 3, halo_up[0], none)
        before_edge = jnp.where(fr > 0, halo_up[1], none)
        current = jnp.concatenate([first, second], axis=0)
        before = jnp.concatenate([before_edge, first], axis=0)
        after = jnp.concatenate([jnp.where(two, second, after_edge), after_edge], axis=0)
        grad = lax.dot_general(current, wbuf[CH : 2 * CH, :], NT, preferred_element_type=jnp.float32)
        grad += lax.dot_general(after, wbuf[0:CH, :], NT, preferred_element_type=jnp.float32)
        grad += lax.dot_general(before, wbuf[2 * CH : 3 * CH, :], NT, preferred_element_type=jnp.float32)
        sgrad[...] = grad.astype(jnp.bfloat16)

    acc[...] = jnp.zeros((2 * PIX, CH), jnp.float32)
    patch_grad[...] = jnp.zeros((2 * PIX, 9 * CH), jnp.float32)

    normalise()
    z(0)
    make_patches()
    z(1)
    x(0)
    y(0)
    local_t.wait()
    local_s.wait()
    arrived(240, orr.at[0])
    arrived(720, orr.at[1])
    forward(plane)
    z(2)
    x(1)
    y(1)
    z(3)
    x(2)
    r(0)
    z(4)
    send_direct()
    r(1)
    y(2)
    z(5)
    x(3)
    y(3)
    z(6)
    x(4)
    r(2)
    from_core(1, 0)
    from_core(2, 0)
    from_core(3, 0)
    spatial_gradient()
    z(7)
    x(5)
    y(4)
    backward(plane)
    r(3)
    y(5)
    take_direct(0)
    x(6)
    r(4)
    from_core(2, 1)
    from_core(2, 2)
    forward(plane_of(2))
    take_direct(1)
    x(7)
    y(6)
    backward(plane_of(2))
    take_direct(2)
    r(5)
    y(7)
    take_direct(3)
    r(6)
    from_core(3, 1)
    from_core(3, 2)
    forward(plane_of(3))
    r(7)
    backward(plane_of(3))
    from_core(1, 1)
    from_core(1, 2)
    forward(plane_of(1))
    spat[...] = acc[...].astype(jnp.bfloat16)
    edge_sp[0] = spat[:PIX, :]
    edge_sp[1] = jnp.where(two, spat[PIX:, :], spat[:PIX, :])
    sp_copies = halo(edge_sp, halo_sp, 2)
    backward(plane_of(1))

    acc[...] = dot32(spat[...], wbuf[CH : 2 * CH, :])

    total = jnp.zeros((2 * PIX, CH), jnp.float32)
    none = jnp.zeros((WW, CH), jnp.float32)
    for dx in range(3):
        def tap(dy, q):
            k = 3 * dy + dx
            return patch_grad[q * WW : (q + 1) * WW, k * CH : (k + 1) * CH]
        parts = []
        for base in (0, 2):
            parts.append(tap(1, base) + tap(0, base + 1))
            parts.append(tap(1, base + 1) + tap(2, base))
        summed = jnp.concatenate(parts, axis=0)
        if dx == 0:
            summed = jnp.where(column == WW - 1, 0.0, pltpu.roll(summed, 2 * PIX - 1, 0))
        elif dx == 2:
            summed = jnp.where(column == 0, 0.0, pltpu.roll(summed, 1, 0))
        total = total + summed
    shifted = shifted_s[...]
    scaled = scaled_s[...]
    sigma = jax.nn.sigmoid(shifted)
    norm_grad = total * sigma * (1.0 + shifted * (1.0 - sigma)) * gain_ref[...].reshape(1, CH)
    sums = frame_sums(norm_grad) + frame_sums(norm_grad * scaled)
    means = group_means(stack8(sums), gather_m, spread_m, size)
    first = on_cells(means[0:1], means[1:2])
    second = on_cells(means[2:3], means[3:4])
    inverse = on_cells(inv_s[0:1, :], inv_s[1:2, :])
    grad = cot_ref[...].astype(jnp.float32) + inverse * (norm_grad - first - scaled * second)
    ig_ref[:PIX, :] = grad[:PIX].astype(jnp.bfloat16)
    ig_ref[PIX:, :] = jnp.where(two, grad[PIX:], 0.0).astype(jnp.bfloat16)

    for copy in sp_copies:
        copy.wait()
    empty = jnp.zeros((PIX, CH), jnp.bfloat16)
    after_edge = jnp.where(fr < 3, halo_sp[0], empty)
    before_edge = jnp.where(fr > 0, halo_sp[1], empty)
    before = jnp.concatenate([before_edge, spat[:PIX, :]], axis=0)
    after = jnp.concatenate([jnp.where(two, spat[PIX:, :], after_edge), after_edge], axis=0)
    temporal = acc[...] + dot32(before, wbuf[0:CH, :]) + dot32(after, wbuf[2 * CH : 3 * CH, :])
    result = lat_ref[...].astype(jnp.float32) + temporal
    out_ref[:PIX, :] = result[:PIX].astype(jnp.bfloat16)
    out_ref[PIX:, :] = jnp.where(two, result[PIX:], 0.0).astype(jnp.bfloat16)
    for lane in range(4):
        view = wbuf.at[pl.ds(0, sent_rows[lane])]
        pltpu.make_async_remote_copy(
            src_ref=view, dst_ref=view, send_sem=sent.at[lane], recv_sem=orr.at[0],
            device_id=(other, fr), device_id_type=MESH,
        ).wait_send()


def fused(latents, lengths, norm_gain, norm_bias, spatial_weight, temporal_weight, cotangent):
    rows = 2 * PIX
    dma = pltpu.SemaphoreType.DMA
    vmem = pl.BlockSpec(memory_space=pltpu.VMEM)
    cells = jax.ShapeDtypeStruct((rows, CH), jnp.bfloat16)
    out, grad = pl.pallas_call(
        kernel,
        out_shape=(cells, cells),
        in_specs=[pl.BlockSpec(memory_space=pltpu.MemorySpace.HBM)] * 7,
        out_specs=(vmem, vmem),
        scratch_shapes=[
            pltpu.SMEM((1, 1), jnp.int32),
            pltpu.VMEM((rows, CH), jnp.bfloat16),
            pltpu.VMEM((rows, CH), jnp.bfloat16),
            pltpu.VMEM((CH,), jnp.float32),
            pltpu.VMEM((CH,), jnp.float32),
            dma((5,)),
            pltpu.VMEM((TROWS + PLANES * CHUNK, CH), jnp.bfloat16),
            pltpu.VMEM((rows, 9 * CH), jnp.bfloat16),
            pltpu.VMEM((rows, 9 * CH), jnp.float32),
            pltpu.VMEM((rows, CH), jnp.float32),
            pltpu.VMEM((rows, CH), jnp.bfloat16),
            pltpu.VMEM((rows, CH), jnp.float32),
            pltpu.VMEM((rows, CH), jnp.float32),
            pltpu.VMEM((8, CH), jnp.float32),
            pltpu.VMEM((rows, CH), jnp.bfloat16),
        ] + [pltpu.VMEM((2, PIX, CH), jnp.bfloat16)] * 4
        + [dma((n,)) for n in (2, 4, 12, 8, 8, 8, 9, 2, 4, 4)],
        compiler_params=pltpu.CompilerParams(
            collective_id=0, has_side_effects=True, vmem_limit_bytes=60 << 20
        ),
    )(
        lengths, latents.reshape(rows, CH), cotangent.reshape(rows, CH),
        norm_gain, norm_bias, spatial_weight, temporal_weight,
    )
    return (out.reshape(latents.shape), grad.reshape(latents.shape))


def solution(mesh):
    in_specs = (
        P("dp", "frames", None, None, None),
        P("dp", "frames"),
        P(),
        P(),
        P("dp", None),
        P("dp", None),
        P("dp", "frames", None, None, None),
    )
    out_specs = (P("dp", "frames", None, None, None), P("dp", "frames", None, None, None))
    small = mesh.shape["dp"] == 2 * PLANES and mesh.shape["frames"] == 4
    body = fused if small else shards
    return jax.shard_map(body, mesh=mesh, in_specs=in_specs, out_specs=out_specs, check_vma=False)
```

```python
import functools

import jax
import jax.numpy as jnp
from jax import lax
from jax.experimental import pallas as pl
from jax.experimental.pallas import tpu as pltpu
from jax.sharding import PartitionSpec as P

CH = 640
GROUPS = 32
HH = 2
WW = 32
PIX = 64


epsilon = 1e-05


def padded_2(cells, sides, width):
    for axis, dim in sides:
        count = lax.axis_size(axis)
        ends = count - 1
        head = lax.slice_in_dim(cells, 0, width, axis=dim)
        tail = lax.slice_in_dim(cells, cells.shape[dim] - width, cells.shape[dim], axis=dim)
        cells = jnp.concatenate(
            [
                lax.ppermute(tail, axis, [(i, (i + 1) % count) for i in range(ends)]),
                cells,
                lax.ppermute(head, axis, [((i + 1) % count, i) for i in range(ends)]),
            ],
            axis=dim,
        )
    return cells


def normalize(frames_in, norm_gain, norm_bias):
    shaped = frames_in.reshape(frames_in.shape[0], -1, GROUPS, CH // GROUPS)
    centre = jnp.mean(shaped, axis=(1, 3), keepdims=True)
    spread = jnp.mean(jnp.square(shaped - centre), axis=(1, 3), keepdims=True)
    inverse = lax.rsqrt(spread + epsilon)
    scaled = (shaped - centre) * inverse
    shifted = scaled.reshape(frames_in.shape) * norm_gain + norm_bias
    return (scaled, inverse, shifted)


def norm_backward(active_grad, scaled, inverse, shifted, norm_gain):
    sigma = jax.nn.sigmoid(shifted)
    shift_grad = active_grad * sigma * (1.0 + shifted * (1.0 - sigma))
    norm_grad = (shift_grad * norm_gain).reshape(scaled.shape)
    first = jnp.mean(norm_grad, axis=(1, 3), keepdims=True)
    second = jnp.mean(norm_grad * scaled, axis=(1, 3), keepdims=True)
    return (inverse * (norm_grad - first - scaled * second)).reshape(active_grad.shape)


def patchify(active):
    padded = jnp.pad(active, ((0, 0), (1, 1), (1, 1), (0, 0)))
    pieces = [padded[:, row : row + HH, col : col + WW, :] for row in range(3) for col in range(3)]
    return jnp.concatenate(pieces, axis=-1).reshape(-1, 9 * CH)


def unpatchify(patch_grad):
    count = patch_grad.shape[0] // (HH * WW)
    shaped = patch_grad.reshape(count, HH, WW, 9, CH)
    total = jnp.zeros((count, HH + 2, WW + 2, CH), jnp.float32)
    for row in range(3):
        for col in range(3):
            total = total + jnp.pad(
                shaped[:, :, :, row * 3 + col, :], ((0, 0), (row, 2 - row), (col, 2 - col), (0, 0))
            )
    return total[:, 1:-1, 1:-1, :]


def contract_rows(left, right):
    return lax.dot_general(
        left, right, (((1,), (1,)), ((), ())), preferred_element_type=jnp.float32
    )


def neighbours(frames_bf, count):
    last_frame = lax.dynamic_index_in_dim(frames_bf, count - 1, 0, keepdims=False)
    boundary = jnp.stack([frames_bf[0], last_frame])
    padded = padded_2(boundary, (("frames", 0),), 1)
    before_frames = jnp.concatenate([padded[0:1], frames_bf[:-1]])
    candidate = jnp.concatenate([frames_bf[1:], padded[3:4]])
    places = jnp.arange(frames_bf.shape[0], dtype=jnp.int32)
    after_frames = jnp.where((places + 1 < count)[:, None, None], candidate, padded[3:4])
    return (before_frames, after_frames)


def shards(latents, lengths, norm_gain, norm_bias, spatial_weight, temporal_weight, cotangent):
    clip_in = latents[0]
    clip_cot = cotangent[0]
    slots_here = clip_in.shape[0]
    count = lengths[0, 0]
    valid = jnp.arange(slots_here, dtype=jnp.int32) < count
    keep = valid[:, None, None, None]
    spatial_full, temporal_full = (
        lax.all_gather(spatial_weight, "dp", axis=0, tiled=True),
        lax.all_gather(temporal_weight, "dp", axis=0, tiled=True),
    )
    first_w = temporal_full[:CH]
    centre_w = temporal_full[CH : 2 * CH]
    last_w = temporal_full[2 * CH :]
    values = clip_in.astype(jnp.float32)
    scaled, inverse, shifted = normalize(values, norm_gain, norm_bias)
    active = jax.nn.silu(shifted).astype(jnp.bfloat16)
    patches = patchify(active)
    spatial = jnp.dot(patches, spatial_full, preferred_element_type=jnp.float32)
    spatial = spatial.astype(jnp.bfloat16).reshape(slots_here, PIX, CH)
    earlier, later_frames = neighbours(spatial, count)
    temporal = jnp.dot(earlier.reshape(-1, CH), first_w, preferred_element_type=jnp.float32)
    temporal = temporal + jnp.dot(
        spatial.reshape(-1, CH), centre_w, preferred_element_type=jnp.float32
    )
    temporal = temporal + jnp.dot(
        later_frames.reshape(-1, CH), last_w, preferred_element_type=jnp.float32
    )
    temporal = temporal.reshape(slots_here, HH, WW, CH)
    output = jnp.where(keep, values + temporal, 0.0).astype(jnp.bfloat16)
    upstream = jnp.where(keep, clip_cot, jnp.zeros_like(clip_cot)).reshape(slots_here, PIX, CH)
    up_before, up_after = neighbours(upstream, count)
    spatial_grad = contract_rows(upstream.reshape(-1, CH), centre_w)
    spatial_grad = spatial_grad + contract_rows(up_after.reshape(-1, CH), first_w)
    spatial_grad = spatial_grad + contract_rows(up_before.reshape(-1, CH), last_w)
    spatial_grad = spatial_grad.astype(jnp.bfloat16)
    patch_grad = contract_rows(spatial_grad, spatial_full)
    active_grad = unpatchify(patch_grad)
    latent_grad = norm_backward(active_grad, scaled, inverse, shifted, norm_gain)
    input_grad = jnp.where(keep, clip_cot.astype(jnp.float32) + latent_grad, 0.0).astype(
        jnp.bfloat16
    )
    return (output[None], input_grad[None])

MESH = pl.DeviceIdType.MESH
BLK = 80
PLANES = 4
TROWS = 3 * CH
CHUNK = 1536
STRIDE = 1408
A, B, C = range(3)
EVENTS = ((A, 0), (B, 0), (C, 0), (B, 1), (B, 2), (C, 1), (C, 2))
PAIRED = (A, 1)
DIRECT = (A, 2)
N_EV = len(EVENTS)
OVER_X = ((0, 1, 4, 5), (1, 4, 5))
END_ORDER = (
    "a", "cE", "H", "U", "z0", "b", "cN", "g0", "g1", "x0", "y0", "z1", "s", "t0", "z2", "y1", "z4", "x2",
    "O", "x1", "z3", "y4", "r0", "y2", "z5", "cM", "r2", "x4", "x3", "z6", "r1", "y3", "cO", "r4",
    "cS", "d1", "y5", "d0", "r3", "t1", "x6", "cV", "x5", "cB", "d2", "d3", "y6", "r5", "r6", "cA",
    "cC", "cT",
)
MID_ORDER = (
    "a", "cE", "H", "F0", "z0", "b", "F1", "z1", "g0", "O", "F2", "y1", "z2", "F3", "x2", "F4", "z4",
    "x1", "x0", "r1", "F5", "z3", "d0", "d1", "y4", "F6", "y2", "r2", "U", "d2", "cN", "x3", "y3",
    "g1", "s", "y0", "x4", "cM", "z5", "r4", "cO", "d3", "z6", "r0", "r3", "cS", "cV", "x6", "t1",
    "y5", "t0", "cB", "y6", "x5", "cA", "r5", "r6", "cC", "cT",
)
NT = (((1,), (1,)), ((), ()))


def row_of(plane, core, block):
    late = (block + 9) // 12
    early_row = (2 * plane + core) * 240 + block * BLK
    late_row = TROWS + plane * (CHUNK + 32) + core * 720 + (block - 3) * BLK
    return pl.multiple_of((1 - late) * early_row + late * late_row, 16)


def split3(rows):
    high = rows.astype(jnp.bfloat16)
    rest = rows - high.astype(jnp.float32)
    mid = rest.astype(jnp.bfloat16)
    low = (rest - mid.astype(jnp.float32)).astype(jnp.bfloat16)
    return high, mid, low


def dot32(left, right):
    return jnp.dot(left, right, preferred_element_type=jnp.float32)


def group_means(rows, gather_m, spread_m, size):
    high, mid, low = split3(rows)
    sums = dot32(high, gather_m) + dot32(mid, gather_m) + dot32(low, gather_m)
    high, mid, low = split3(sums * (1.0 / size))
    return dot32(high, spread_m) + dot32(mid, spread_m) + dot32(low, spread_m)


def frame_sums(cells):
    return tuple(
        jnp.sum(cells[at : at + PIX], axis=0, keepdims=True) for at in range(0, cells.shape[0], PIX)
    )


def stack8(rows):
    return jnp.concatenate(list(rows) + [jnp.zeros((8 - len(rows), CH), jnp.float32)], axis=0)


def on_cells(rows):
    return jnp.concatenate(
        [jnp.broadcast_to(rows[n : n + 1], (PIX, CH)) for n in range(rows.shape[0])], axis=0
    )


def kernel(
    len_hbm, lat_hbm, cot_hbm, gain_hbm, bias_hbm, ws_ref, wt_ref,
    out_ref, ig_ref,
    len_ref, lat_ref, cot_ref, gain_ref, bias_ref, in_sem, wbuf, patches, patch_grad, acc, sgrad, scaled_s, shifted_s, inv_s, spat, edge_up, edge_lat, halo_up,
    own_sem, sent, zr, xr, yr, rr, pr, orr, hs, hr,
):
    me = lax.axis_index("dp")
    fr = lax.axis_index("frames")
    plane = me // 2
    core = me % 2
    other = me + 1 - 2 * core
    fx = fr + 1 - 2 * (fr % 2)
    fy = (fr + 2) % 4
    fd = 3 - fr
    right = (fr + 1) % 4
    left = (fr + 3) % 4

    mid = (plane + 1) // 2 % 2
    is_mid = mid == 1
    pair = plane + 1 - 2 * (plane % 2)
    inner = 2 - plane // 2
    outer = 3 - 3 * (plane // 2)
    across = 3 - plane

    def plane_of(slot):
        return (pair, inner, outer)[slot]

    barrier = pltpu.get_barrier_semaphore()
    pl.semaphore_signal(barrier, inc=1, device_id=(2 * pair + core, fr), device_id_type=MESH)

    @pl.when(is_mid)
    def _():
        pl.semaphore_signal(barrier, inc=1, device_id=(2 * across + core, fr), device_id_type=MESH)

    for f in (fx, fy):
        pl.semaphore_signal(barrier, inc=1, device_id=(me, f), device_id_type=MESH)
    centre = (fr + 1) // 2 % 2

    @pl.when(centre == 1)
    def _():
        pl.semaphore_signal(barrier, inc=1, device_id=(me, fd), device_id_type=MESH)

    pl.semaphore_signal(barrier, inc=1, device_id=(other, fr), device_id_type=MESH)

    own_t = pl.multiple_of(me * 240, 16)
    own_s = pl.multiple_of(TROWS + plane * (CHUNK + 32) + core * 720, 16)
    inputs = [
        pltpu.make_async_copy(src, dst, in_sem.at[n])
        for n, (src, dst) in enumerate(
            ((len_hbm, len_ref), (cot_hbm, cot_ref), (lat_hbm, lat_ref.at[0 : 2 * PIX]), (gain_hbm, gain_ref), (bias_hbm, bias_ref))
        )
    ]
    for copy in inputs:
        copy.start()
    local_t = pltpu.make_async_copy(wt_ref, wbuf.at[pl.ds(own_t, 240)], own_sem.at[0])
    local_s = pltpu.make_async_copy(ws_ref, wbuf.at[pl.ds(own_s, 720)], own_sem.at[1])
    local_t.start()
    local_s.start()

    for p in range(PLANES):
        base = TROWS + p * CHUNK
        if p > 0:
            wbuf[base : base + 32 * p, :] = jnp.zeros((32 * p, CH), jnp.bfloat16)
        if p < 3:
            wbuf[base + 1440 + 32 * p : base + CHUNK, :] = jnp.zeros((96 - 32 * p, CH), jnp.bfloat16)

    @pl.when(fr == 0)
    def _():
        lat_ref[2 * PIX : 3 * PIX, :] = jnp.zeros((PIX, CH), jnp.bfloat16)
        halo_up[0] = jnp.zeros((PIX, CH), jnp.bfloat16)

    @pl.when(fr == 3)
    def _():
        lat_ref[3 * PIX :, :] = jnp.zeros((PIX, CH), jnp.bfloat16)
        halo_up[1] = jnp.zeros((PIX, CH), jnp.bfloat16)

    pl.semaphore_wait(barrier, 4 + mid + centre)

    def send(src, row, count, lane, recv_sem, device):
        view = wbuf.at[pl.ds(row, count)]
        pltpu.make_async_remote_copy(
            src_ref=view if src is None else src, dst_ref=view, send_sem=sent.at[lane], recv_sem=recv_sem,
            device_id=device, device_id_type=MESH,
        ).start()

    def arrived(count, recv_sem):
        view = wbuf.at[pl.ds(0, count)]
        pltpu.make_async_remote_copy(
            src_ref=view, dst_ref=view, send_sem=sent.at[0], recv_sem=recv_sem,
            device_id=(other, fr), device_id_type=MESH,
        ).wait_recv()

    def halo(edge, dest, k):
        return [
            pltpu.make_async_remote_copy(
                src_ref=edge.at[side], dst_ref=dest[side], send_sem=hs.at[k + side],
                recv_sem=hr.at[k + side], device_id=(me, device), device_id_type=MESH,
            )
            for side, device in ((0, right), (1, left))
        ]

    def halo_start(copies):
        pl.when(fr < 3)(copies[0].start)
        pl.when(fr > 0)(copies[1].start)

    def halo_arrived(copies):
        pl.when(fr > 0)(copies[0].wait_recv)
        pl.when(fr < 3)(copies[1].wait_recv)

    def halo_sent(copies):
        pl.when(fr < 3)(copies[0].wait_send)
        pl.when(fr > 0)(copies[1].wait_send)

    def z_send(p, view, src, recv_sem):
        pltpu.make_async_remote_copy(
            src_ref=src, dst_ref=view, send_sem=sent.at[0], recv_sem=recv_sem,
            device_id=(2 * p + core, fr), device_id_type=MESH,
        ).start()

    def z_sem(slot, j):
        return zr.at[EVENTS.index((slot, j))]

    def z_own(p, j, f, recv_sem):
        view = wbuf.at[pl.ds(row_of(plane, core, 4 * j + f), BLK)]
        if j > 0:
            at = pl.multiple_of((4 * j + f - 3) * BLK, 16)
            z_send(p, view, ws_ref.at[pl.ds(at, BLK)], recv_sem)
            return

        @pl.when(f < 3)
        def _():
            z_send(p, view, wt_ref.at[pl.ds(pl.multiple_of((f % 3) * BLK, 16), BLK)], recv_sem)

        @pl.when(f == 3)
        def _():
            z_send(p, view, ws_ref.at[pl.ds(0, BLK)], recv_sem)

    def across_from_pair(j, row):
        view = wbuf.at[pl.ds(row, BLK)]
        z_send(across, view, view, z_sem(C, j))
        if j < 2:
            z_own(across, j + 1, fr, z_sem(B, j + 1))

    def to_core(row, k, j):
        send(None, row, BLK, 3, pr.at[3 * k + j], (other, fr))

    def event_row(e, f):
        k, j = EVENTS[e]
        return row_of(plane_of(k), core, 4 * j + f)

    centre_column = centre == 1

    def over_x(e, value):
        routes = [(e in OVER_X[n]) == value for n in range(2)]
        if routes[0] == routes[1]:
            return routes[0]
        return centre_column if routes[1] else jnp.logical_not(centre_column)

    def relay(condition, row, lane, e, device):
        def go():
            send(None, row, BLK, lane, rr.at[e], device)

        if condition is True:
            go()
        elif condition is not False:
            pl.when(condition)(go)

    def act_a(n, middle):
        z_own(pair, 0, fr, z_sem(A, 0))
        if middle:
            z_own(across, 0, fr, z_sem(B, 0))

    def act_b(n, middle):
        for g, f in enumerate((fr, fx)):
            z_own(pair, 1, f, zr.at[N_EV + g])

    def act_s(n, middle):
        for d in range(4):
            z_own(pair, 2, (fr + d) % 4, zr.at[N_EV + 2 + d])

    def act_O(n, middle):
        send(wt_ref, own_t, 240, 3, orr.at[0], (other, fr))
        send(ws_ref, own_s, 720, 3, orr.at[1], (other, fr))

    def act_H(n, middle):
        halo_start(lat_copies)

    def act_U(n, middle):
        halo_start(up_copies)

    def act_F(e, middle):
        k, j = EVENTS[e]
        row = event_row(e, fr)
        arrived(BLK, zr.at[e])
        if k == A:
            across_from_pair(j, row)
        else:
            z_send(pair, wbuf.at[pl.ds(row, BLK)], wbuf.at[pl.ds(row, BLK)], z_sem(k, j))

    def act_z(e, middle):
        row = event_row(e, fr)
        if not middle:
            arrived(BLK, zr.at[e])
        send(None, row, BLK, 1, xr.at[e], (me, fx))
        send(None, row, BLK, 2, yr.at[e], (me, fy))
        to_core(row, *EVENTS[e])

    def act_x(e, middle):
        row = event_row(e, fx)
        arrived(BLK, xr.at[e])
        relay(over_x(e, False), row, 2, e, (me, fy))
        to_core(row, *EVENTS[e])

    def act_y(e, middle):
        row = event_row(e, fy)
        arrived(BLK, yr.at[e])
        relay(over_x(e, True), row, 1, e, (me, fx))
        to_core(row, *EVENTS[e])

    def act_r(e, middle):
        arrived(BLK, rr.at[e])
        to_core(event_row(e, fd), *EVENTS[e])

    def act_g(n, middle):
        row = row_of(pair, core, 4 * PAIRED[1] + (fr, fx)[n])
        arrived(BLK, zr.at[N_EV + n])
        if n == 0 and middle:
            across_from_pair(PAIRED[1], row)
        send(None, row, BLK, 2, yr.at[N_EV + n], (me, fy))
        to_core(row, *PAIRED)

    def act_t(n, middle):
        arrived(BLK, yr.at[N_EV + n])
        to_core(row_of(pair, core, 4 * PAIRED[1] + (fy, fd)[n]), *PAIRED)

    def act_d(n, middle):
        row = row_of(pair, core, 4 * DIRECT[1] + (fr + n) % 4)
        arrived(BLK, zr.at[N_EV + 2 + n])
        if n == 0 and middle:
            across_from_pair(DIRECT[1], row)
        to_core(row, *DIRECT)

    actions = {
        "a": act_a, "b": act_b, "s": act_s, "O": act_O, "H": act_H, "U": act_U, "F": act_F, "z": act_z,
        "x": act_x, "y": act_y, "r": act_r, "g": act_g, "t": act_t, "d": act_d,
    }
    orders = [list(END_ORDER), list(MID_ORDER)]

    def run(until):
        def steps(middle):
            order = orders[middle]
            while order and order[0] != until:
                name = order.pop(0)
                actions[name[0]](int(name[1:] or 0), middle)
            if order:
                order.pop(0)

        pl.when(mid == 0)(lambda: steps(False))
        pl.when(is_mid)(lambda: steps(True))

    run("cE")
    inputs[0].wait()
    inputs[1].wait()
    two = len_ref[0, 0] > 1
    cot_bf = cot_ref[...]
    edge_up[0] = jnp.where(two, cot_bf[PIX:], cot_bf[:PIX])
    edge_up[1] = cot_bf[:PIX]
    inputs[2].wait()
    lat_bf = lat_ref[: 2 * PIX, :]
    edge_lat[0] = jnp.where(two, lat_bf[PIX:], lat_bf[:PIX])
    edge_lat[1] = lat_bf[:PIX]
    lat_copies = halo(edge_lat, (lat_ref.at[2 * PIX : 3 * PIX], lat_ref.at[3 * PIX : 4 * PIX]), 0)
    up_copies = halo(edge_up, (halo_up.at[0], halo_up.at[1]), 2)

    def from_core(k, j):
        arrived(4 * BLK, pr.at[3 * k + j])

    def chunk_rows(p):
        return pl.ds(pl.multiple_of(TROWS + p * CHUNK, 128), CHUNK)

    def chunk_lanes(p):
        return pl.ds(pl.multiple_of(p * STRIDE, 128), CHUNK)

    def forward(p):
        acc[...] += dot32(patches[:, chunk_lanes(p)], wbuf[chunk_rows(p), :])

    def backward(p):
        grad = lax.dot_general(
            sgrad[...], wbuf[chunk_rows(p), :], NT, preferred_element_type=jnp.float32
        )
        patch_grad[:, chunk_lanes(p)] += grad

    channel = lax.broadcasted_iota(jnp.int32, (CH, 128), 0)
    group = lax.broadcasted_iota(jnp.int32, (CH, 128), 1) * (CH // GROUPS)
    gather_m = ((channel >= group) & (channel < group + CH // GROUPS)).astype(jnp.float32).astype(jnp.bfloat16)
    channel = lax.broadcasted_iota(jnp.int32, (128, CH), 1)
    group = lax.broadcasted_iota(jnp.int32, (128, CH), 0) * (CH // GROUPS)
    spread_m = ((channel >= group) & (channel < group + CH // GROUPS)).astype(jnp.float32).astype(jnp.bfloat16)
    size = PIX * (CH // GROUPS)

    column = lax.broadcasted_iota(jnp.int32, (4 * PIX, CH), 0) % WW

    def normalise():
        for copy in inputs[3:]:
            copy.wait()
        halo_arrived(lat_copies)
        values = lat_ref[...].astype(jnp.float32)
        centre = group_means(stack8(frame_sums(values)), gather_m, spread_m, size)
        centred = values - on_cells(centre[0:4])
        spread = group_means(stack8(frame_sums(centred * centred)), gather_m, spread_m, size)
        inverse = lax.rsqrt(spread + epsilon)
        inv_s[...] = inverse
        scaled = centred * on_cells(inverse[0:4])
        scaled_s[...] = scaled[: 2 * PIX]
        shifted_s[...] = scaled * gain_ref[...].reshape(1, CH) + bias_ref[...].reshape(1, CH)

    def make_patches():
        shifted = shifted_s[...]
        active = (shifted * jax.nn.sigmoid(shifted)).astype(jnp.bfloat16).astype(jnp.float32)
        zero = jnp.zeros((WW, CH), jnp.bfloat16)
        for dx in range(3):
            if dx == 1:
                moved = active
            elif dx == 0:
                moved = jnp.where(column == 0, 0.0, pltpu.roll(active, 1, 0))
            else:
                moved = jnp.where(column == WW - 1, 0.0, pltpu.roll(active, 4 * PIX - 1, 0))
            moved = moved.astype(jnp.bfloat16)
            quarters = [moved[q * WW : (q + 1) * WW] for q in range(8)]
            for dy in range(3):
                lanes = slice((3 * dy + dx) * CH, (3 * dy + dx + 1) * CH)
                for q in range(8):
                    if dy == 1:
                        rows = quarters[q]
                    elif dy == 0:
                        rows = quarters[q - 1] if q % 2 else zero
                    else:
                        rows = zero if q % 2 else quarters[q + 1]
                    patches[q * WW : (q + 1) * WW, lanes] = rows

    def spatial_gradient():
        halo_arrived(up_copies)
        first, second = cot_bf[:PIX], cot_bf[PIX:]
        none = jnp.zeros((PIX, CH), jnp.bfloat16)
        second = jnp.where(two, second, none)
        before_edge = halo_up[0]
        after_edge = halo_up[1]
        current = jnp.concatenate([first, second], axis=0)
        before = jnp.concatenate([before_edge, first], axis=0)
        after = jnp.concatenate([jnp.where(two, second, after_edge), after_edge], axis=0)
        grad = lax.dot_general(current, wbuf[CH : 2 * CH, :], NT, preferred_element_type=jnp.float32)
        grad += lax.dot_general(after, wbuf[0:CH, :], NT, preferred_element_type=jnp.float32)
        grad += lax.dot_general(before, wbuf[2 * CH : 3 * CH, :], NT, preferred_element_type=jnp.float32)
        sgrad[...] = grad.astype(jnp.bfloat16)

    acc[...] = jnp.zeros((4 * PIX, CH), jnp.float32)
    patch_grad[...] = jnp.zeros((2 * PIX, 9 * CH), jnp.float32)

    run("cN")
    normalise()
    run("cM")
    make_patches()
    run("cO")
    local_t.wait()
    local_s.wait()
    arrived(240, orr.at[0])
    arrived(720, orr.at[1])
    forward(plane)
    run("cS")
    from_core(A, 0)
    from_core(B, 0)
    from_core(C, 0)
    spatial_gradient()
    run("cV")
    backward(plane)
    run("cB")
    from_core(B, 1)
    from_core(B, 2)
    forward(plane_of(B))
    backward(plane_of(B))
    run("cA")
    from_core(A, 1)
    from_core(A, 2)
    forward(plane_of(A))
    backward(plane_of(A))
    run("cC")
    from_core(C, 1)
    from_core(C, 2)
    forward(plane_of(C))
    run("cT")
    spat[...] = acc[...].astype(jnp.bfloat16)
    backward(plane_of(C))

    total = jnp.zeros((2 * PIX, CH), jnp.float32)
    none = jnp.zeros((WW, CH), jnp.float32)
    for dx in range(3):
        def tap(dy, q):
            k = 3 * dy + dx
            return patch_grad[q * WW : (q + 1) * WW, k * CH : (k + 1) * CH]
        parts = []
        for base in (0, 2):
            parts.append(tap(1, base) + tap(0, base + 1))
            parts.append(tap(1, base + 1) + tap(2, base))
        summed = jnp.concatenate(parts, axis=0)
        if dx == 0:
            summed = jnp.where(column[: 2 * PIX] == WW - 1, 0.0, pltpu.roll(summed, 2 * PIX - 1, 0))
        elif dx == 2:
            summed = jnp.where(column[: 2 * PIX] == 0, 0.0, pltpu.roll(summed, 1, 0))
        total = total + summed
    shifted = shifted_s[: 2 * PIX, :]
    scaled = scaled_s[...]
    sigma = jax.nn.sigmoid(shifted)
    norm_grad = total * sigma * (1.0 + shifted * (1.0 - sigma)) * gain_ref[...].reshape(1, CH)
    sums = frame_sums(norm_grad) + frame_sums(norm_grad * scaled)
    means = group_means(stack8(sums), gather_m, spread_m, size)
    first = on_cells(means[0:2])
    second = on_cells(means[2:4])
    inverse = on_cells(inv_s[0:2, :])
    grad = cot_ref[...].astype(jnp.float32) + inverse * (norm_grad - first - scaled * second)
    ig_ref[:PIX, :] = grad[:PIX].astype(jnp.bfloat16)
    ig_ref[PIX:, :] = jnp.where(two, grad[PIX:], 0.0).astype(jnp.bfloat16)

    empty = jnp.zeros((PIX, CH), jnp.bfloat16)
    before_edge = jnp.where(fr > 0, spat[2 * PIX : 3 * PIX, :], empty)
    after_edge = jnp.where(fr < 3, spat[3 * PIX :, :], empty)
    before = jnp.concatenate([before_edge, spat[:PIX, :]], axis=0)
    after = jnp.concatenate([jnp.where(two, spat[PIX : 2 * PIX, :], after_edge), after_edge], axis=0)
    temporal = dot32(before, wbuf[0:CH, :]) + dot32(spat[: 2 * PIX, :], wbuf[CH : 2 * CH, :])
    temporal += dot32(after, wbuf[2 * CH : 3 * CH, :])
    result = lat_ref[: 2 * PIX, :].astype(jnp.float32) + temporal
    out_ref[:PIX, :] = result[:PIX].astype(jnp.bfloat16)
    out_ref[PIX:, :] = jnp.where(two, result[PIX:], 0.0).astype(jnp.bfloat16)
    halo_sent(lat_copies)
    halo_sent(up_copies)

    def all_sent(lane, count):
        view = wbuf.at[pl.ds(0, count)]
        pltpu.make_async_remote_copy(
            src_ref=view, dst_ref=view, send_sem=sent.at[lane], recv_sem=orr.at[0],
            device_id=(other, fr), device_id_type=MESH,
        ).wait_send()

    all_sent(0, 7 * BLK)
    pl.when(is_mid)(lambda: all_sent(0, 12 * BLK))
    for n, here in ((0, jnp.logical_not(centre_column)), (1, centre_column)):
        turned = len(OVER_X[n])
        pl.when(here)(lambda turned=turned: all_sent(1, (N_EV + turned) * BLK))
        pl.when(here)(lambda turned=turned: all_sent(2, (2 * N_EV + 2 - turned) * BLK))
    all_sent(3, 48 * BLK)


def fused(latents, lengths, norm_gain, norm_bias, spatial_weight, temporal_weight, cotangent):
    rows = 2 * PIX
    dma = pltpu.SemaphoreType.DMA
    vmem = pl.BlockSpec(memory_space=pltpu.VMEM)
    cells = jax.ShapeDtypeStruct((rows, CH), jnp.bfloat16)
    out, grad = pl.pallas_call(
        kernel,
        out_shape=(cells, cells),
        in_specs=[pl.BlockSpec(memory_space=pltpu.MemorySpace.HBM)] * 7,
        out_specs=(vmem, vmem),
        scratch_shapes=[
            pltpu.SMEM((1, 1), jnp.int32),
            pltpu.VMEM((2 * rows, CH), jnp.bfloat16),
            pltpu.VMEM((rows, CH), jnp.bfloat16),
            pltpu.VMEM((CH,), jnp.float32),
            pltpu.VMEM((CH,), jnp.float32),
            dma((5,)),
            pltpu.VMEM((TROWS + PLANES * CHUNK, CH), jnp.bfloat16),
            pltpu.VMEM((2 * rows, 9 * CH), jnp.bfloat16),
            pltpu.VMEM((rows, 9 * CH), jnp.float32),
            pltpu.VMEM((2 * rows, CH), jnp.float32),
            pltpu.VMEM((rows, CH), jnp.bfloat16),
            pltpu.VMEM((rows, CH), jnp.float32),
            pltpu.VMEM((2 * rows, CH), jnp.float32),
            pltpu.VMEM((8, CH), jnp.float32),
            pltpu.VMEM((2 * rows, CH), jnp.bfloat16),
        ] + [pltpu.VMEM((2, PIX, CH), jnp.bfloat16)] * 3
        + [dma((n,)) for n in (2, 4, N_EV + 6, N_EV, N_EV + 2, N_EV, 9, 2, 4, 4)],
        compiler_params=pltpu.CompilerParams(
            collective_id=0, has_side_effects=True, vmem_limit_bytes=60 << 20
        ),
    )(
        lengths, latents.reshape(rows, CH), cotangent.reshape(rows, CH),
        norm_gain, norm_bias, spatial_weight, temporal_weight,
    )
    return (out.reshape(latents.shape), grad.reshape(latents.shape))


def solution(mesh):
    in_specs = (
        P("dp", "frames", None, None, None),
        P("dp", "frames"),
        P(),
        P(),
        P("dp", None),
        P("dp", None),
        P("dp", "frames", None, None, None),
    )
    out_specs = (P("dp", "frames", None, None, None), P("dp", "frames", None, None, None))
    small = mesh.shape["dp"] == 2 * PLANES and mesh.shape["frames"] == 4
    body = fused if small else shards
    return jax.shard_map(body, mesh=mesh, in_specs=in_specs, out_specs=out_specs, check_vma=False)
```

```python
import functools

import jax
import jax.numpy as jnp
from jax import lax
from jax.experimental import pallas as pl
from jax.experimental.pallas import tpu as pltpu
from jax.sharding import PartitionSpec as P

CH = 640
GROUPS = 32
HH = 2
WW = 32
PIX = 64


epsilon = 1e-05


def padded_2(cells, sides, width):
    for axis, dim in sides:
        count = lax.axis_size(axis)
        ends = count - 1
        head = lax.slice_in_dim(cells, 0, width, axis=dim)
        tail = lax.slice_in_dim(cells, cells.shape[dim] - width, cells.shape[dim], axis=dim)
        cells = jnp.concatenate(
            [
                lax.ppermute(tail, axis, [(i, (i + 1) % count) for i in range(ends)]),
                cells,
                lax.ppermute(head, axis, [((i + 1) % count, i) for i in range(ends)]),
            ],
            axis=dim,
        )
    return cells


def normalize(frames_in, norm_gain, norm_bias):
    shaped = frames_in.reshape(frames_in.shape[0], -1, GROUPS, CH // GROUPS)
    centre = jnp.mean(shaped, axis=(1, 3), keepdims=True)
    spread = jnp.mean(jnp.square(shaped - centre), axis=(1, 3), keepdims=True)
    inverse = lax.rsqrt(spread + epsilon)
    scaled = (shaped - centre) * inverse
    shifted = scaled.reshape(frames_in.shape) * norm_gain + norm_bias
    return (scaled, inverse, shifted)


def norm_backward(active_grad, scaled, inverse, shifted, norm_gain):
    sigma = jax.nn.sigmoid(shifted)
    shift_grad = active_grad * sigma * (1.0 + shifted * (1.0 - sigma))
    norm_grad = (shift_grad * norm_gain).reshape(scaled.shape)
    first = jnp.mean(norm_grad, axis=(1, 3), keepdims=True)
    second = jnp.mean(norm_grad * scaled, axis=(1, 3), keepdims=True)
    return (inverse * (norm_grad - first - scaled * second)).reshape(active_grad.shape)


def patchify(active):
    padded = jnp.pad(active, ((0, 0), (1, 1), (1, 1), (0, 0)))
    pieces = [padded[:, row : row + HH, col : col + WW, :] for row in range(3) for col in range(3)]
    return jnp.concatenate(pieces, axis=-1).reshape(-1, 9 * CH)


def unpatchify(patch_grad):
    count = patch_grad.shape[0] // (HH * WW)
    shaped = patch_grad.reshape(count, HH, WW, 9, CH)
    total = jnp.zeros((count, HH + 2, WW + 2, CH), jnp.float32)
    for row in range(3):
        for col in range(3):
            total = total + jnp.pad(
                shaped[:, :, :, row * 3 + col, :], ((0, 0), (row, 2 - row), (col, 2 - col), (0, 0))
            )
    return total[:, 1:-1, 1:-1, :]


def contract_rows(left, right):
    return lax.dot_general(
        left, right, (((1,), (1,)), ((), ())), preferred_element_type=jnp.float32
    )


def neighbours(frames_bf, count):
    last_frame = lax.dynamic_index_in_dim(frames_bf, count - 1, 0, keepdims=False)
    boundary = jnp.stack([frames_bf[0], last_frame])
    padded = padded_2(boundary, (("frames", 0),), 1)
    before_frames = jnp.concatenate([padded[0:1], frames_bf[:-1]])
    candidate = jnp.concatenate([frames_bf[1:], padded[3:4]])
    places = jnp.arange(frames_bf.shape[0], dtype=jnp.int32)
    after_frames = jnp.where((places + 1 < count)[:, None, None], candidate, padded[3:4])
    return (before_frames, after_frames)


def shards(latents, lengths, norm_gain, norm_bias, spatial_weight, temporal_weight, cotangent):
    clip_in = latents[0]
    clip_cot = cotangent[0]
    slots_here = clip_in.shape[0]
    count = lengths[0, 0]
    valid = jnp.arange(slots_here, dtype=jnp.int32) < count
    keep = valid[:, None, None, None]
    spatial_full, temporal_full = (
        lax.all_gather(spatial_weight, "dp", axis=0, tiled=True),
        lax.all_gather(temporal_weight, "dp", axis=0, tiled=True),
    )
    first_w = temporal_full[:CH]
    centre_w = temporal_full[CH : 2 * CH]
    last_w = temporal_full[2 * CH :]
    values = clip_in.astype(jnp.float32)
    scaled, inverse, shifted = normalize(values, norm_gain, norm_bias)
    active = jax.nn.silu(shifted).astype(jnp.bfloat16)
    patches = patchify(active)
    spatial = jnp.dot(patches, spatial_full, preferred_element_type=jnp.float32)
    spatial = spatial.astype(jnp.bfloat16).reshape(slots_here, PIX, CH)
    earlier, later_frames = neighbours(spatial, count)
    temporal = jnp.dot(earlier.reshape(-1, CH), first_w, preferred_element_type=jnp.float32)
    temporal = temporal + jnp.dot(
        spatial.reshape(-1, CH), centre_w, preferred_element_type=jnp.float32
    )
    temporal = temporal + jnp.dot(
        later_frames.reshape(-1, CH), last_w, preferred_element_type=jnp.float32
    )
    temporal = temporal.reshape(slots_here, HH, WW, CH)
    output = jnp.where(keep, values + temporal, 0.0).astype(jnp.bfloat16)
    upstream = jnp.where(keep, clip_cot, jnp.zeros_like(clip_cot)).reshape(slots_here, PIX, CH)
    up_before, up_after = neighbours(upstream, count)
    spatial_grad = contract_rows(upstream.reshape(-1, CH), centre_w)
    spatial_grad = spatial_grad + contract_rows(up_after.reshape(-1, CH), first_w)
    spatial_grad = spatial_grad + contract_rows(up_before.reshape(-1, CH), last_w)
    spatial_grad = spatial_grad.astype(jnp.bfloat16)
    patch_grad = contract_rows(spatial_grad, spatial_full)
    active_grad = unpatchify(patch_grad)
    latent_grad = norm_backward(active_grad, scaled, inverse, shifted, norm_gain)
    input_grad = jnp.where(keep, clip_cot.astype(jnp.float32) + latent_grad, 0.0).astype(
        jnp.bfloat16
    )
    return (output[None], input_grad[None])

MESH = pl.DeviceIdType.MESH
BLK = 80
PLANES = 4
TROWS = 3 * CH
CHUNK = 1536
STRIDE = 1408
A, B, C = range(3)
EVENTS = ((A, 0), (B, 0), (C, 0), (B, 1), (B, 2), (C, 1), (C, 2))
PAIRED = (A, 1)
DIRECT = (A, 2)
N_EV = len(EVENTS)
OVER_X = ((0, 1, 4, 5), (1, 4, 5))
END_ORDER = (
    "a", "cE", "H", "U", "z0", "b", "cN", "g0", "g1", "x0", "y0", "z1", "s", "t0", "z2", "y1", "z4", "x2",
    "O", "x1", "z3", "y4", "r0", "y2", "z5", "cM", "r2", "x4", "x3", "z6", "r1", "y3", "cO", "r4",
    "cS", "d1", "y5", "d0", "r3", "t1", "x6", "cV", "x5", "cB", "d2", "d3", "y6", "r5", "r6", "cA",
    "cC", "cT",
)
MID_ORDER = (
    "a", "cE", "H", "F0", "z0", "b", "F1", "z1", "g0", "O", "F2", "y1", "z2", "F3", "x2", "F4", "z4",
    "x1", "x0", "r1", "F5", "z3", "d0", "d1", "y4", "F6", "y2", "r2", "U", "d2", "cN", "x3", "y3",
    "g1", "s", "y0", "x4", "cM", "z5", "r4", "cO", "d3", "z6", "r0", "r3", "cS", "cV", "x6", "t1",
    "y5", "t0", "cB", "y6", "x5", "cA", "r5", "r6", "cC", "cT",
)
NT = (((1,), (1,)), ((), ()))


def row_of(plane, core, block):
    late = (block + 9) // 12
    early_row = (2 * plane + core) * 240 + block * BLK
    late_row = TROWS + plane * (CHUNK + 32) + core * 720 + (block - 3) * BLK
    return pl.multiple_of((1 - late) * early_row + late * late_row, 16)


def split3(rows):
    high = rows.astype(jnp.bfloat16)
    rest = rows - high.astype(jnp.float32)
    mid = rest.astype(jnp.bfloat16)
    low = (rest - mid.astype(jnp.float32)).astype(jnp.bfloat16)
    return high, mid, low


def dot32(left, right):
    return jnp.dot(left, right, preferred_element_type=jnp.float32)


def group_means(rows, gather_m, spread_m, size):
    high, mid, low = split3(rows)
    sums = dot32(high, gather_m) + dot32(mid, gather_m) + dot32(low, gather_m)
    high, mid, low = split3(sums * (1.0 / size))
    return dot32(high, spread_m) + dot32(mid, spread_m) + dot32(low, spread_m)


def frame_sums(cells):
    return tuple(
        jnp.sum(cells[at : at + PIX], axis=0, keepdims=True) for at in range(0, cells.shape[0], PIX)
    )


def stack8(rows):
    return jnp.concatenate(list(rows) + [jnp.zeros((8 - len(rows), CH), jnp.float32)], axis=0)


def on_cells(rows):
    return jnp.concatenate(
        [jnp.broadcast_to(rows[n : n + 1], (PIX, CH)) for n in range(rows.shape[0])], axis=0
    )


def kernel(
    len_hbm, lat_hbm, cot_hbm, gain_hbm, bias_hbm, ws_ref, wt_ref,
    out_any, ig_any,
    len_ref, lat_ref, cot_ref, gain_ref, bias_ref, in_sem, wbuf, patches, patch_grad, acc, sgrad, scaled_s, shifted_s, inv_s, spat, out_ref, ig_ref, out_sem, edge_up, edge_lat, halo_up,
    own_sem, sent, zr, xr, yr, rr, pr, orr, hs, hr,
):
    me = lax.axis_index("dp")
    fr = lax.axis_index("frames")
    plane = me // 2
    core = me % 2
    other = me + 1 - 2 * core
    fx = fr + 1 - 2 * (fr % 2)
    fy = (fr + 2) % 4
    fd = 3 - fr
    right = (fr + 1) % 4
    left = (fr + 3) % 4

    mid = (plane + 1) // 2 % 2
    is_mid = mid == 1
    pair = plane + 1 - 2 * (plane % 2)
    inner = 2 - plane // 2
    outer = 3 - 3 * (plane // 2)
    across = 3 - plane

    def plane_of(slot):
        return (pair, inner, outer)[slot]

    barrier = pltpu.get_barrier_semaphore()
    pl.semaphore_signal(barrier, inc=1, device_id=(2 * pair + core, fr), device_id_type=MESH)

    @pl.when(is_mid)
    def _():
        pl.semaphore_signal(barrier, inc=1, device_id=(2 * across + core, fr), device_id_type=MESH)

    for f in (fx, fy):
        pl.semaphore_signal(barrier, inc=1, device_id=(me, f), device_id_type=MESH)
    centre = (fr + 1) // 2 % 2

    @pl.when(centre == 1)
    def _():
        pl.semaphore_signal(barrier, inc=1, device_id=(me, fd), device_id_type=MESH)

    pl.semaphore_signal(barrier, inc=1, device_id=(other, fr), device_id_type=MESH)

    own_t = pl.multiple_of(me * 240, 16)
    own_s = pl.multiple_of(TROWS + plane * (CHUNK + 32) + core * 720, 16)
    inputs = [
        pltpu.make_async_copy(src, dst, in_sem.at[n])
        for n, (src, dst) in enumerate(
            ((len_hbm, len_ref), (cot_hbm, cot_ref), (lat_hbm, lat_ref.at[0 : 2 * PIX]), (gain_hbm, gain_ref), (bias_hbm, bias_ref))
        )
    ]
    for copy in inputs:
        copy.start()
    local_t = pltpu.make_async_copy(wt_ref, wbuf.at[pl.ds(own_t, 240)], own_sem.at[0])
    local_s = pltpu.make_async_copy(ws_ref, wbuf.at[pl.ds(own_s, 720)], own_sem.at[1])
    local_t.start()
    local_s.start()

    for p in range(PLANES):
        base = TROWS + p * CHUNK
        if p > 0:
            wbuf[base : base + 32 * p, :] = jnp.zeros((32 * p, CH), jnp.bfloat16)
        if p < 3:
            wbuf[base + 1440 + 32 * p : base + CHUNK, :] = jnp.zeros((96 - 32 * p, CH), jnp.bfloat16)

    @pl.when(fr == 0)
    def _():
        lat_ref[2 * PIX : 3 * PIX, :] = jnp.zeros((PIX, CH), jnp.bfloat16)
        halo_up[0] = jnp.zeros((PIX, CH), jnp.bfloat16)

    @pl.when(fr == 3)
    def _():
        lat_ref[3 * PIX :, :] = jnp.zeros((PIX, CH), jnp.bfloat16)
        halo_up[1] = jnp.zeros((PIX, CH), jnp.bfloat16)

    pl.semaphore_wait(barrier, 4 + mid + centre)

    def send(src, row, count, lane, recv_sem, device):
        view = wbuf.at[pl.ds(row, count)]
        pltpu.make_async_remote_copy(
            src_ref=view if src is None else src, dst_ref=view, send_sem=sent.at[lane], recv_sem=recv_sem,
            device_id=device, device_id_type=MESH,
        ).start()

    def arrived(count, recv_sem):
        view = wbuf.at[pl.ds(0, count)]
        pltpu.make_async_remote_copy(
            src_ref=view, dst_ref=view, send_sem=sent.at[0], recv_sem=recv_sem,
            device_id=(other, fr), device_id_type=MESH,
        ).wait_recv()

    def halo(edge, dest, k):
        return [
            pltpu.make_async_remote_copy(
                src_ref=edge.at[side], dst_ref=dest[side], send_sem=hs.at[k + side],
                recv_sem=hr.at[k + side], device_id=(me, device), device_id_type=MESH,
            )
            for side, device in ((0, right), (1, left))
        ]

    def halo_start(copies):
        pl.when(fr < 3)(copies[0].start)
        pl.when(fr > 0)(copies[1].start)

    def halo_arrived(copies):
        pl.when(fr > 0)(copies[0].wait_recv)
        pl.when(fr < 3)(copies[1].wait_recv)

    def halo_sent(copies):
        pl.when(fr < 3)(copies[0].wait_send)
        pl.when(fr > 0)(copies[1].wait_send)

    def z_send(p, view, src, recv_sem):
        pltpu.make_async_remote_copy(
            src_ref=src, dst_ref=view, send_sem=sent.at[0], recv_sem=recv_sem,
            device_id=(2 * p + core, fr), device_id_type=MESH,
        ).start()

    def z_sem(slot, j):
        return zr.at[EVENTS.index((slot, j))]

    def z_own(p, j, f, recv_sem):
        view = wbuf.at[pl.ds(row_of(plane, core, 4 * j + f), BLK)]
        if j > 0:
            at = pl.multiple_of((4 * j + f - 3) * BLK, 16)
            z_send(p, view, ws_ref.at[pl.ds(at, BLK)], recv_sem)
            return

        @pl.when(f < 3)
        def _():
            z_send(p, view, wt_ref.at[pl.ds(pl.multiple_of((f % 3) * BLK, 16), BLK)], recv_sem)

        @pl.when(f == 3)
        def _():
            z_send(p, view, ws_ref.at[pl.ds(0, BLK)], recv_sem)

    def across_from_pair(j, row):
        view = wbuf.at[pl.ds(row, BLK)]
        z_send(across, view, view, z_sem(C, j))
        if j < 2:
            z_own(across, j + 1, fr, z_sem(B, j + 1))

    def to_core(row, k, j):
        send(None, row, BLK, 3, pr.at[3 * k + j], (other, fr))

    def event_row(e, f):
        k, j = EVENTS[e]
        return row_of(plane_of(k), core, 4 * j + f)

    centre_column = centre == 1

    def over_x(e, value):
        routes = [(e in OVER_X[n]) == value for n in range(2)]
        if routes[0] == routes[1]:
            return routes[0]
        return centre_column if routes[1] else jnp.logical_not(centre_column)

    def relay(condition, row, lane, e, device):
        def go():
            send(None, row, BLK, lane, rr.at[e], device)

        if condition is True:
            go()
        elif condition is not False:
            pl.when(condition)(go)

    def act_a(n, middle):
        z_own(pair, 0, fr, z_sem(A, 0))
        if middle:
            z_own(across, 0, fr, z_sem(B, 0))

    def act_b(n, middle):
        for g, f in enumerate((fr, fx)):
            z_own(pair, 1, f, zr.at[N_EV + g])

    def act_s(n, middle):
        for d in range(4):
            z_own(pair, 2, (fr + d) % 4, zr.at[N_EV + 2 + d])

    def act_O(n, middle):
        send(wt_ref, own_t, 240, 3, orr.at[0], (other, fr))
        send(ws_ref, own_s, 720, 3, orr.at[1], (other, fr))

    def act_H(n, middle):
        halo_start(lat_copies)

    def act_U(n, middle):
        halo_start(up_copies)

    def act_F(e, middle):
        k, j = EVENTS[e]
        row = event_row(e, fr)
        arrived(BLK, zr.at[e])
        if k == A:
            across_from_pair(j, row)
        else:
            z_send(pair, wbuf.at[pl.ds(row, BLK)], wbuf.at[pl.ds(row, BLK)], z_sem(k, j))

    def act_z(e, middle):
        row = event_row(e, fr)
        if not middle:
            arrived(BLK, zr.at[e])
        send(None, row, BLK, 1, xr.at[e], (me, fx))
        send(None, row, BLK, 2, yr.at[e], (me, fy))
        to_core(row, *EVENTS[e])

    def act_x(e, middle):
        row = event_row(e, fx)
        arrived(BLK, xr.at[e])
        relay(over_x(e, False), row, 2, e, (me, fy))
        to_core(row, *EVENTS[e])

    def act_y(e, middle):
        row = event_row(e, fy)
        arrived(BLK, yr.at[e])
        relay(over_x(e, True), row, 1, e, (me, fx))
        to_core(row, *EVENTS[e])

    def act_r(e, middle):
        arrived(BLK, rr.at[e])
        to_core(event_row(e, fd), *EVENTS[e])

    def act_g(n, middle):
        row = row_of(pair, core, 4 * PAIRED[1] + (fr, fx)[n])
        arrived(BLK, zr.at[N_EV + n])
        if n == 0 and middle:
            across_from_pair(PAIRED[1], row)
        send(None, row, BLK, 2, yr.at[N_EV + n], (me, fy))
        to_core(row, *PAIRED)

    def act_t(n, middle):
        arrived(BLK, yr.at[N_EV + n])
        to_core(row_of(pair, core, 4 * PAIRED[1] + (fy, fd)[n]), *PAIRED)

    def act_d(n, middle):
        row = row_of(pair, core, 4 * DIRECT[1] + (fr + n) % 4)
        arrived(BLK, zr.at[N_EV + 2 + n])
        if n == 0 and middle:
            across_from_pair(DIRECT[1], row)
        to_core(row, *DIRECT)

    actions = {
        "a": act_a, "b": act_b, "s": act_s, "O": act_O, "H": act_H, "U": act_U, "F": act_F, "z": act_z,
        "x": act_x, "y": act_y, "r": act_r, "g": act_g, "t": act_t, "d": act_d,
    }
    orders = [list(END_ORDER), list(MID_ORDER)]

    def run(until):
        def steps(middle):
            order = orders[middle]
            while order and order[0] != until:
                name = order.pop(0)
                actions[name[0]](int(name[1:] or 0), middle)
            if order:
                order.pop(0)

        pl.when(mid == 0)(lambda: steps(False))
        pl.when(is_mid)(lambda: steps(True))

    run("cE")
    inputs[0].wait()
    inputs[1].wait()
    two = len_ref[0, 0] > 1
    cot_bf = cot_ref[...]
    edge_up[0] = jnp.where(two, cot_bf[PIX:], cot_bf[:PIX])
    edge_up[1] = cot_bf[:PIX]
    inputs[2].wait()
    lat_bf = lat_ref[: 2 * PIX, :]
    edge_lat[0] = jnp.where(two, lat_bf[PIX:], lat_bf[:PIX])
    edge_lat[1] = lat_bf[:PIX]
    lat_copies = halo(edge_lat, (lat_ref.at[2 * PIX : 3 * PIX], lat_ref.at[3 * PIX : 4 * PIX]), 0)
    up_copies = halo(edge_up, (halo_up.at[0], halo_up.at[1]), 2)

    def from_core(k, j):
        arrived(4 * BLK, pr.at[3 * k + j])

    def chunk_rows(p):
        return pl.ds(pl.multiple_of(TROWS + p * CHUNK, 128), CHUNK)

    def chunk_lanes(p):
        return pl.ds(pl.multiple_of(p * STRIDE, 128), CHUNK)

    def forward(p):
        acc[...] += dot32(patches[:, chunk_lanes(p)], wbuf[chunk_rows(p), :])

    def backward(p):
        grad = lax.dot_general(
            sgrad[...], wbuf[chunk_rows(p), :], NT, preferred_element_type=jnp.float32
        )
        patch_grad[:, chunk_lanes(p)] += grad

    channel = lax.broadcasted_iota(jnp.int32, (CH, 128), 0)
    group = lax.broadcasted_iota(jnp.int32, (CH, 128), 1) * (CH // GROUPS)
    gather_m = ((channel >= group) & (channel < group + CH // GROUPS)).astype(jnp.float32).astype(jnp.bfloat16)
    channel = lax.broadcasted_iota(jnp.int32, (128, CH), 1)
    group = lax.broadcasted_iota(jnp.int32, (128, CH), 0) * (CH // GROUPS)
    spread_m = ((channel >= group) & (channel < group + CH // GROUPS)).astype(jnp.float32).astype(jnp.bfloat16)
    size = PIX * (CH // GROUPS)

    column = lax.broadcasted_iota(jnp.int32, (4 * PIX, CH), 0) % WW

    def normalise():
        for copy in inputs[3:]:
            copy.wait()
        halo_arrived(lat_copies)
        values = lat_ref[...].astype(jnp.float32)
        centre = group_means(stack8(frame_sums(values)), gather_m, spread_m, size)
        centred = values - on_cells(centre[0:4])
        spread = group_means(stack8(frame_sums(centred * centred)), gather_m, spread_m, size)
        inverse = lax.rsqrt(spread + epsilon)
        inv_s[...] = inverse
        scaled = centred * on_cells(inverse[0:4])
        scaled_s[...] = scaled[: 2 * PIX]
        shifted_s[...] = scaled * gain_ref[...].reshape(1, CH) + bias_ref[...].reshape(1, CH)

    def make_patches():
        shifted = shifted_s[...]
        active = (shifted * jax.nn.sigmoid(shifted)).astype(jnp.bfloat16).astype(jnp.float32)
        zero = jnp.zeros((WW, CH), jnp.bfloat16)
        for dx in range(3):
            if dx == 1:
                moved = active
            elif dx == 0:
                moved = jnp.where(column == 0, 0.0, pltpu.roll(active, 1, 0))
            else:
                moved = jnp.where(column == WW - 1, 0.0, pltpu.roll(active, 4 * PIX - 1, 0))
            moved = moved.astype(jnp.bfloat16)
            quarters = [moved[q * WW : (q + 1) * WW] for q in range(8)]
            for dy in range(3):
                lanes = slice((3 * dy + dx) * CH, (3 * dy + dx + 1) * CH)
                for q in range(8):
                    if dy == 1:
                        rows = quarters[q]
                    elif dy == 0:
                        rows = quarters[q - 1] if q % 2 else zero
                    else:
                        rows = zero if q % 2 else quarters[q + 1]
                    patches[q * WW : (q + 1) * WW, lanes] = rows

    def spatial_gradient():
        halo_arrived(up_copies)
        first, second = cot_bf[:PIX], cot_bf[PIX:]
        none = jnp.zeros((PIX, CH), jnp.bfloat16)
        second = jnp.where(two, second, none)
        before_edge = halo_up[0]
        after_edge = halo_up[1]
        current = jnp.concatenate([first, second], axis=0)
        before = jnp.concatenate([before_edge, first], axis=0)
        after = jnp.concatenate([jnp.where(two, second, after_edge), after_edge], axis=0)
        grad = lax.dot_general(current, wbuf[CH : 2 * CH, :], NT, preferred_element_type=jnp.float32)
        grad += lax.dot_general(after, wbuf[0:CH, :], NT, preferred_element_type=jnp.float32)
        grad += lax.dot_general(before, wbuf[2 * CH : 3 * CH, :], NT, preferred_element_type=jnp.float32)
        sgrad[...] = grad.astype(jnp.bfloat16)

    acc[...] = jnp.zeros((4 * PIX, CH), jnp.float32)
    patch_grad[...] = jnp.zeros((2 * PIX, 9 * CH), jnp.float32)

    run("cN")
    normalise()
    run("cM")
    make_patches()
    run("cO")
    local_t.wait()
    local_s.wait()
    arrived(240, orr.at[0])
    arrived(720, orr.at[1])
    forward(plane)
    run("cS")
    from_core(A, 0)
    from_core(B, 0)
    from_core(C, 0)
    spatial_gradient()
    run("cV")
    backward(plane)
    run("cB")
    from_core(B, 1)
    from_core(B, 2)
    forward(plane_of(B))
    backward(plane_of(B))
    run("cA")
    from_core(A, 1)
    from_core(A, 2)
    forward(plane_of(A))
    backward(plane_of(A))
    run("cC")
    from_core(C, 1)
    from_core(C, 2)
    forward(plane_of(C))
    run("cT")
    spat[...] = acc[...].astype(jnp.bfloat16)
    backward(plane_of(C))

    total = jnp.zeros((2 * PIX, CH), jnp.float32)
    none = jnp.zeros((WW, CH), jnp.float32)
    for dx in range(3):
        def tap(dy, q):
            k = 3 * dy + dx
            return patch_grad[q * WW : (q + 1) * WW, k * CH : (k + 1) * CH]
        parts = []
        for base in (0, 2):
            parts.append(tap(1, base) + tap(0, base + 1))
            parts.append(tap(1, base + 1) + tap(2, base))
        summed = jnp.concatenate(parts, axis=0)
        if dx == 0:
            summed = jnp.where(column[: 2 * PIX] == WW - 1, 0.0, pltpu.roll(summed, 2 * PIX - 1, 0))
        elif dx == 2:
            summed = jnp.where(column[: 2 * PIX] == 0, 0.0, pltpu.roll(summed, 1, 0))
        total = total + summed
    shifted = shifted_s[: 2 * PIX, :]
    scaled = scaled_s[...]
    sigma = jax.nn.sigmoid(shifted)
    norm_grad = total * sigma * (1.0 + shifted * (1.0 - sigma)) * gain_ref[...].reshape(1, CH)
    sums = frame_sums(norm_grad) + frame_sums(norm_grad * scaled)
    means = group_means(stack8(sums), gather_m, spread_m, size)
    first = on_cells(means[0:2])
    second = on_cells(means[2:4])
    inverse = on_cells(inv_s[0:2, :])
    grad = cot_ref[...].astype(jnp.float32) + inverse * (norm_grad - first - scaled * second)
    ig_ref[:PIX, :] = grad[:PIX].astype(jnp.bfloat16)
    ig_ref[PIX:, :] = jnp.where(two, grad[PIX:], 0.0).astype(jnp.bfloat16)

    ig_copy = pltpu.make_async_copy(ig_ref, ig_any, out_sem.at[0])
    ig_copy.start()

    empty = jnp.zeros((PIX, CH), jnp.bfloat16)
    before_edge = jnp.where(fr > 0, spat[2 * PIX : 3 * PIX, :], empty)
    after_edge = jnp.where(fr < 3, spat[3 * PIX :, :], empty)
    before = jnp.concatenate([before_edge, spat[:PIX, :]], axis=0)
    after = jnp.concatenate([jnp.where(two, spat[PIX : 2 * PIX, :], after_edge), after_edge], axis=0)
    temporal = dot32(before, wbuf[0:CH, :]) + dot32(spat[: 2 * PIX, :], wbuf[CH : 2 * CH, :])
    temporal += dot32(after, wbuf[2 * CH : 3 * CH, :])
    result = lat_ref[: 2 * PIX, :].astype(jnp.float32) + temporal
    out_ref[:PIX, :] = result[:PIX].astype(jnp.bfloat16)
    out_ref[PIX:, :] = jnp.where(two, result[PIX:], 0.0).astype(jnp.bfloat16)
    out_copy = pltpu.make_async_copy(out_ref, out_any, out_sem.at[1])
    out_copy.start()
    halo_sent(lat_copies)
    halo_sent(up_copies)

    def all_sent(lane, count):
        view = wbuf.at[pl.ds(0, count)]
        pltpu.make_async_remote_copy(
            src_ref=view, dst_ref=view, send_sem=sent.at[lane], recv_sem=orr.at[0],
            device_id=(other, fr), device_id_type=MESH,
        ).wait_send()

    all_sent(0, 7 * BLK)
    pl.when(is_mid)(lambda: all_sent(0, 12 * BLK))
    for n, here in ((0, jnp.logical_not(centre_column)), (1, centre_column)):
        turned = len(OVER_X[n])
        pl.when(here)(lambda turned=turned: all_sent(1, (N_EV + turned) * BLK))
        pl.when(here)(lambda turned=turned: all_sent(2, (2 * N_EV + 2 - turned) * BLK))
    all_sent(3, 48 * BLK)
    ig_copy.wait()
    out_copy.wait()


def fused(latents, lengths, norm_gain, norm_bias, spatial_weight, temporal_weight, cotangent):
    rows = 2 * PIX
    dma = pltpu.SemaphoreType.DMA
    cells = jax.ShapeDtypeStruct((rows, CH), jnp.bfloat16)
    out, grad = pl.pallas_call(
        kernel,
        out_shape=(cells, cells),
        in_specs=[pl.BlockSpec(memory_space=pltpu.MemorySpace.HBM)] * 7,
        out_specs=(pl.BlockSpec(memory_space=pl.ANY), pl.BlockSpec(memory_space=pl.ANY)),
        scratch_shapes=[
            pltpu.SMEM((1, 1), jnp.int32),
            pltpu.VMEM((2 * rows, CH), jnp.bfloat16),
            pltpu.VMEM((rows, CH), jnp.bfloat16),
            pltpu.VMEM((CH,), jnp.float32),
            pltpu.VMEM((CH,), jnp.float32),
            dma((5,)),
            pltpu.VMEM((TROWS + PLANES * CHUNK, CH), jnp.bfloat16),
            pltpu.VMEM((2 * rows, 9 * CH), jnp.bfloat16),
            pltpu.VMEM((rows, 9 * CH), jnp.float32),
            pltpu.VMEM((2 * rows, CH), jnp.float32),
            pltpu.VMEM((rows, CH), jnp.bfloat16),
            pltpu.VMEM((rows, CH), jnp.float32),
            pltpu.VMEM((2 * rows, CH), jnp.float32),
            pltpu.VMEM((8, CH), jnp.float32),
            pltpu.VMEM((2 * rows, CH), jnp.bfloat16),
            pltpu.VMEM((rows, CH), jnp.bfloat16),
            pltpu.VMEM((rows, CH), jnp.bfloat16),
            dma((2,)),
        ] + [pltpu.VMEM((2, PIX, CH), jnp.bfloat16)] * 3
        + [dma((n,)) for n in (2, 4, N_EV + 6, N_EV, N_EV + 2, N_EV, 9, 2, 4, 4)],
        compiler_params=pltpu.CompilerParams(
            collective_id=0, has_side_effects=True, vmem_limit_bytes=107 << 19
        ),
    )(
        lengths, latents.reshape(rows, CH), cotangent.reshape(rows, CH),
        norm_gain, norm_bias, spatial_weight, temporal_weight,
    )
    return (out.reshape(latents.shape), grad.reshape(latents.shape))


def solution(mesh):
    in_specs = (
        P("dp", "frames", None, None, None),
        P("dp", "frames"),
        P(),
        P(),
        P("dp", None),
        P("dp", None),
        P("dp", "frames", None, None, None),
    )
    out_specs = (P("dp", "frames", None, None, None), P("dp", "frames", None, None, None))
    small = mesh.shape["dp"] == 2 * PLANES and mesh.shape["frames"] == 4
    body = fused if small else shards
    return jax.shard_map(body, mesh=mesh, in_specs=in_specs, out_specs=out_specs, check_vma=False)
```

```python
import functools

import jax
import jax.numpy as jnp
from jax import lax
from jax.experimental import pallas as pl
from jax.experimental.pallas import tpu as pltpu
from jax.sharding import PartitionSpec as P

CH = 640
GROUPS = 32
HH = 2
WW = 32
PIX = 64


epsilon = 1e-05


def padded_2(cells, sides, width):
    for axis, dim in sides:
        count = lax.axis_size(axis)
        ends = count - 1
        head = lax.slice_in_dim(cells, 0, width, axis=dim)
        tail = lax.slice_in_dim(cells, cells.shape[dim] - width, cells.shape[dim], axis=dim)
        cells = jnp.concatenate(
            [
                lax.ppermute(tail, axis, [(i, (i + 1) % count) for i in range(ends)]),
                cells,
                lax.ppermute(head, axis, [((i + 1) % count, i) for i in range(ends)]),
            ],
            axis=dim,
        )
    return cells


def normalize(frames_in, norm_gain, norm_bias):
    shaped = frames_in.reshape(frames_in.shape[0], -1, GROUPS, CH // GROUPS)
    centre = jnp.mean(shaped, axis=(1, 3), keepdims=True)
    spread = jnp.mean(jnp.square(shaped - centre), axis=(1, 3), keepdims=True)
    inverse = lax.rsqrt(spread + epsilon)
    scaled = (shaped - centre) * inverse
    shifted = scaled.reshape(frames_in.shape) * norm_gain + norm_bias
    return (scaled, inverse, shifted)


def norm_backward(active_grad, scaled, inverse, shifted, norm_gain):
    sigma = jax.nn.sigmoid(shifted)
    shift_grad = active_grad * sigma * (1.0 + shifted * (1.0 - sigma))
    norm_grad = (shift_grad * norm_gain).reshape(scaled.shape)
    first = jnp.mean(norm_grad, axis=(1, 3), keepdims=True)
    second = jnp.mean(norm_grad * scaled, axis=(1, 3), keepdims=True)
    return (inverse * (norm_grad - first - scaled * second)).reshape(active_grad.shape)


def patchify(active):
    padded = jnp.pad(active, ((0, 0), (1, 1), (1, 1), (0, 0)))
    pieces = [padded[:, row : row + HH, col : col + WW, :] for row in range(3) for col in range(3)]
    return jnp.concatenate(pieces, axis=-1).reshape(-1, 9 * CH)


def unpatchify(patch_grad):
    count = patch_grad.shape[0] // (HH * WW)
    shaped = patch_grad.reshape(count, HH, WW, 9, CH)
    total = jnp.zeros((count, HH + 2, WW + 2, CH), jnp.float32)
    for row in range(3):
        for col in range(3):
            total = total + jnp.pad(
                shaped[:, :, :, row * 3 + col, :], ((0, 0), (row, 2 - row), (col, 2 - col), (0, 0))
            )
    return total[:, 1:-1, 1:-1, :]


def contract_rows(left, right):
    return lax.dot_general(
        left, right, (((1,), (1,)), ((), ())), preferred_element_type=jnp.float32
    )


def neighbours(frames_bf, count):
    last_frame = lax.dynamic_index_in_dim(frames_bf, count - 1, 0, keepdims=False)
    boundary = jnp.stack([frames_bf[0], last_frame])
    padded = padded_2(boundary, (("frames", 0),), 1)
    before_frames = jnp.concatenate([padded[0:1], frames_bf[:-1]])
    candidate = jnp.concatenate([frames_bf[1:], padded[3:4]])
    places = jnp.arange(frames_bf.shape[0], dtype=jnp.int32)
    after_frames = jnp.where((places + 1 < count)[:, None, None], candidate, padded[3:4])
    return (before_frames, after_frames)


def shards(latents, lengths, norm_gain, norm_bias, spatial_weight, temporal_weight, cotangent):
    clip_in = latents[0]
    clip_cot = cotangent[0]
    slots_here = clip_in.shape[0]
    count = lengths[0, 0]
    valid = jnp.arange(slots_here, dtype=jnp.int32) < count
    keep = valid[:, None, None, None]
    spatial_full, temporal_full = (
        lax.all_gather(spatial_weight, "dp", axis=0, tiled=True),
        lax.all_gather(temporal_weight, "dp", axis=0, tiled=True),
    )
    first_w = temporal_full[:CH]
    centre_w = temporal_full[CH : 2 * CH]
    last_w = temporal_full[2 * CH :]
    values = clip_in.astype(jnp.float32)
    scaled, inverse, shifted = normalize(values, norm_gain, norm_bias)
    active = jax.nn.silu(shifted).astype(jnp.bfloat16)
    patches = patchify(active)
    spatial = jnp.dot(patches, spatial_full, preferred_element_type=jnp.float32)
    spatial = spatial.astype(jnp.bfloat16).reshape(slots_here, PIX, CH)
    earlier, later_frames = neighbours(spatial, count)
    temporal = jnp.dot(earlier.reshape(-1, CH), first_w, preferred_element_type=jnp.float32)
    temporal = temporal + jnp.dot(
        spatial.reshape(-1, CH), centre_w, preferred_element_type=jnp.float32
    )
    temporal = temporal + jnp.dot(
        later_frames.reshape(-1, CH), last_w, preferred_element_type=jnp.float32
    )
    temporal = temporal.reshape(slots_here, HH, WW, CH)
    output = jnp.where(keep, values + temporal, 0.0).astype(jnp.bfloat16)
    upstream = jnp.where(keep, clip_cot, jnp.zeros_like(clip_cot)).reshape(slots_here, PIX, CH)
    up_before, up_after = neighbours(upstream, count)
    spatial_grad = contract_rows(upstream.reshape(-1, CH), centre_w)
    spatial_grad = spatial_grad + contract_rows(up_after.reshape(-1, CH), first_w)
    spatial_grad = spatial_grad + contract_rows(up_before.reshape(-1, CH), last_w)
    spatial_grad = spatial_grad.astype(jnp.bfloat16)
    patch_grad = contract_rows(spatial_grad, spatial_full)
    active_grad = unpatchify(patch_grad)
    latent_grad = norm_backward(active_grad, scaled, inverse, shifted, norm_gain)
    input_grad = jnp.where(keep, clip_cot.astype(jnp.float32) + latent_grad, 0.0).astype(
        jnp.bfloat16
    )
    return (output[None], input_grad[None])

MESH = pl.DeviceIdType.MESH
BLK = 80
PLANES = 4
TROWS = 3 * CH
CHUNK = 1536
STRIDE = 1408
A, B, C = range(3)
EVENTS = ((A, 0), (B, 0), (C, 0), (B, 1), (B, 2), (C, 1), (C, 2))
PAIRED = (A, 1)
DIRECT = (A, 2)
N_EV = len(EVENTS)
OVER_X = ((0, 1, 4, 5), (0, 1, 4, 5))
END_ORDER = (
    "a", "cE", "U", "b", "z0", "g0", "s", "H", "g1", "y0", "z1", "cN", "z2", "z3", "cM", "z4", "r0",
    "y1", "x0", "O", "x1", "x2", "cO", "x3", "z5", "z6", "y4", "r2", "r1", "y2", "cS", "x4", "cV",
    "y3", "x6", "t0", "x5", "y5", "r3", "r4", "y6", "d2", "d0", "d3", "d1", "t1", "cB", "r6", "r5",
    "cA", "cC", "cT",
)
MID_ORDER = (
    "a", "cE", "q", "b", "H", "F0", "z0", "F1", "g0", "z1", "F2", "z2", "F3", "y0", "d0", "z3",
    "d1", "F4", "y1", "cN", "x0", "z4", "cM", "F5", "x2", "g1", "U", "O", "F6", "cO", "s", "x1",
    "z5", "x3", "d2", "t0", "z6", "y4", "r0", "r1", "r2", "y3", "y2", "cS", "x4", "d3", "t1", "x5",
    "y5", "x6", "cV", "r3", "r4", "y6", "cB", "r5", "r6", "cA", "cC", "cT",
)
NT = (((1,), (1,)), ((), ()))


def row_of(plane, core, block):
    late = (block + 9) // 12
    early_row = (2 * plane + core) * 240 + block * BLK
    late_row = TROWS + plane * (CHUNK + 32) + core * 720 + (block - 3) * BLK
    return pl.multiple_of((1 - late) * early_row + late * late_row, 16)


def split3(rows):
    high = rows.astype(jnp.bfloat16)
    rest = rows - high.astype(jnp.float32)
    mid = rest.astype(jnp.bfloat16)
    low = (rest - mid.astype(jnp.float32)).astype(jnp.bfloat16)
    return high, mid, low


def dot32(left, right):
    return jnp.dot(left, right, preferred_element_type=jnp.float32)


def group_means(rows, gather_m, spread_m, size):
    high, mid, low = split3(rows)
    sums = dot32(high, gather_m) + dot32(mid, gather_m) + dot32(low, gather_m)
    high, mid, low = split3(sums * (1.0 / size))
    return dot32(high, spread_m) + dot32(mid, spread_m) + dot32(low, spread_m)


def frame_sums(cells):
    return tuple(
        jnp.sum(cells[at : at + PIX], axis=0, keepdims=True) for at in range(0, cells.shape[0], PIX)
    )


def stack8(rows):
    return jnp.concatenate(list(rows) + [jnp.zeros((8 - len(rows), CH), jnp.float32)], axis=0)


def on_cells(rows):
    return jnp.concatenate(
        [jnp.broadcast_to(rows[n : n + 1], (PIX, CH)) for n in range(rows.shape[0])], axis=0
    )


def kernel(
    len_hbm, lat_hbm, cot_hbm, gain_hbm, bias_hbm, ws_ref, wt_ref,
    out_any, ig_any,
    len_ref, lat_ref, cot_ref, gain_ref, bias_ref, in_sem, wbuf, patches, patch_grad, acc, sgrad, scaled_s, shifted_s, inv_s, slope_s, spat, out_ref, ig_ref, out_sem, edge_up, edge_lat, halo_up,
    own_sem, sent, zr, xr, yr, rr, pr, orr, hs, hr,
):
    me = lax.axis_index("dp")
    fr = lax.axis_index("frames")
    plane = me // 2
    core = me % 2
    other = me + 1 - 2 * core
    fx = fr + 1 - 2 * (fr % 2)
    fy = (fr + 2) % 4
    fd = 3 - fr
    right = (fr + 1) % 4
    left = (fr + 3) % 4

    mid = (plane + 1) // 2 % 2
    is_mid = mid == 1
    pair = plane + 1 - 2 * (plane % 2)
    inner = 2 - plane // 2
    outer = 3 - 3 * (plane // 2)
    across = 3 - plane

    def plane_of(slot):
        return (pair, inner, outer)[slot]

    barrier = pltpu.get_barrier_semaphore()
    pl.semaphore_signal(barrier, inc=1, device_id=(2 * pair + core, fr), device_id_type=MESH)

    @pl.when(is_mid)
    def _():
        pl.semaphore_signal(barrier, inc=1, device_id=(2 * across + core, fr), device_id_type=MESH)

    for f in (fx, fy):
        pl.semaphore_signal(barrier, inc=1, device_id=(me, f), device_id_type=MESH)
    centre = (fr + 1) // 2 % 2

    @pl.when(centre == 1)
    def _():
        pl.semaphore_signal(barrier, inc=1, device_id=(me, fd), device_id_type=MESH)

    pl.semaphore_signal(barrier, inc=1, device_id=(other, fr), device_id_type=MESH)

    own_t = pl.multiple_of(me * 240, 16)
    own_s = pl.multiple_of(TROWS + plane * (CHUNK + 32) + core * 720, 16)
    inputs = [
        pltpu.make_async_copy(src, dst, in_sem.at[n])
        for n, (src, dst) in enumerate(
            ((len_hbm, len_ref), (cot_hbm, cot_ref), (lat_hbm, lat_ref.at[0 : 2 * PIX]), (gain_hbm, gain_ref), (bias_hbm, bias_ref))
        )
    ]
    for copy in inputs:
        copy.start()
    local_t = pltpu.make_async_copy(wt_ref, wbuf.at[pl.ds(own_t, 240)], own_sem.at[0])
    local_s = pltpu.make_async_copy(ws_ref, wbuf.at[pl.ds(own_s, 720)], own_sem.at[1])
    local_t.start()
    local_s.start()

    for p in range(PLANES):
        base = TROWS + p * CHUNK
        if p > 0:
            wbuf[base : base + 32 * p, :] = jnp.zeros((32 * p, CH), jnp.bfloat16)
        if p < 3:
            wbuf[base + 1440 + 32 * p : base + CHUNK, :] = jnp.zeros((96 - 32 * p, CH), jnp.bfloat16)

    @pl.when(fr == 0)
    def _():
        lat_ref[2 * PIX : 3 * PIX, :] = jnp.zeros((PIX, CH), jnp.bfloat16)
        halo_up[0] = jnp.zeros((PIX, CH), jnp.bfloat16)

    @pl.when(fr == 3)
    def _():
        lat_ref[3 * PIX :, :] = jnp.zeros((PIX, CH), jnp.bfloat16)
        halo_up[1] = jnp.zeros((PIX, CH), jnp.bfloat16)

    pl.semaphore_wait(barrier, 4 + mid + centre)

    def send(src, row, count, lane, recv_sem, device):
        view = wbuf.at[pl.ds(row, count)]
        pltpu.make_async_remote_copy(
            src_ref=view if src is None else src, dst_ref=view, send_sem=sent.at[lane], recv_sem=recv_sem,
            device_id=device, device_id_type=MESH,
        ).start()

    def arrived(count, recv_sem):
        view = wbuf.at[pl.ds(0, count)]
        pltpu.make_async_remote_copy(
            src_ref=view, dst_ref=view, send_sem=sent.at[0], recv_sem=recv_sem,
            device_id=(other, fr), device_id_type=MESH,
        ).wait_recv()

    def halo(edge, dest, k):
        return [
            pltpu.make_async_remote_copy(
                src_ref=edge.at[side], dst_ref=dest[side], send_sem=hs.at[k + side],
                recv_sem=hr.at[k + side], device_id=(me, device), device_id_type=MESH,
            )
            for side, device in ((0, right), (1, left))
        ]

    def halo_start(copies):
        pl.when(fr < 3)(copies[0].start)
        pl.when(fr > 0)(copies[1].start)

    def halo_arrived(copies):
        pl.when(fr > 0)(copies[0].wait_recv)
        pl.when(fr < 3)(copies[1].wait_recv)

    def halo_sent(copies):
        pl.when(fr < 3)(copies[0].wait_send)
        pl.when(fr > 0)(copies[1].wait_send)

    def z_send(p, view, src, recv_sem):
        pltpu.make_async_remote_copy(
            src_ref=src, dst_ref=view, send_sem=sent.at[0], recv_sem=recv_sem,
            device_id=(2 * p + core, fr), device_id_type=MESH,
        ).start()

    def z_sem(slot, j):
        return zr.at[EVENTS.index((slot, j))]

    def z_own(p, j, f, recv_sem):
        view = wbuf.at[pl.ds(row_of(plane, core, 4 * j + f), BLK)]
        if j > 0:
            at = pl.multiple_of((4 * j + f - 3) * BLK, 16)
            z_send(p, view, ws_ref.at[pl.ds(at, BLK)], recv_sem)
            return

        @pl.when(f < 3)
        def _():
            z_send(p, view, wt_ref.at[pl.ds(pl.multiple_of((f % 3) * BLK, 16), BLK)], recv_sem)

        @pl.when(f == 3)
        def _():
            z_send(p, view, ws_ref.at[pl.ds(0, BLK)], recv_sem)

    def across_from_pair(j, row):
        view = wbuf.at[pl.ds(row, BLK)]
        z_send(across, view, view, z_sem(C, j))
        if j < 2:
            z_own(across, j + 1, fr, z_sem(B, j + 1))

    def to_core(row, k, j):
        send(None, row, BLK, 3, pr.at[3 * k + j], (other, fr))

    def event_row(e, f):
        k, j = EVENTS[e]
        return row_of(plane_of(k), core, 4 * j + f)

    centre_column = centre == 1

    def over_x(e, value):
        routes = [(e in OVER_X[n]) == value for n in range(2)]
        if routes[0] == routes[1]:
            return routes[0]
        return centre_column if routes[1] else jnp.logical_not(centre_column)

    def relay(condition, row, lane, e, device):
        def go():
            send(None, row, BLK, lane, rr.at[e], device)

        if condition is True:
            go()
        elif condition is not False:
            pl.when(condition)(go)

    def act_a(n, middle):
        z_own(pair, 0, fr, z_sem(A, 0))

    def act_q(n, middle):
        z_own(across, 0, fr, z_sem(B, 0))

    def act_b(n, middle):
        for g, f in enumerate((fr, fx)):
            z_own(pair, 1, f, zr.at[N_EV + g])

    def act_s(n, middle):
        for d in range(4):
            z_own(pair, 2, (fr + d) % 4, zr.at[N_EV + 2 + d])

    def act_O(n, middle):
        send(wt_ref, own_t, 240, 3, orr.at[0], (other, fr))
        send(ws_ref, own_s, 720, 3, orr.at[1], (other, fr))

    def act_H(n, middle):
        halo_start(lat_copies)

    def act_U(n, middle):
        halo_start(up_copies)

    def act_F(e, middle):
        k, j = EVENTS[e]
        row = event_row(e, fr)
        arrived(BLK, zr.at[e])
        if k == A:
            across_from_pair(j, row)
        else:
            z_send(pair, wbuf.at[pl.ds(row, BLK)], wbuf.at[pl.ds(row, BLK)], z_sem(k, j))

    def act_z(e, middle):
        row = event_row(e, fr)
        if not middle:
            arrived(BLK, zr.at[e])
        send(None, row, BLK, 1, xr.at[e], (me, fx))
        send(None, row, BLK, 2, yr.at[e], (me, fy))
        to_core(row, *EVENTS[e])

    def act_x(e, middle):
        row = event_row(e, fx)
        arrived(BLK, xr.at[e])
        relay(over_x(e, False), row, 2, e, (me, fy))
        to_core(row, *EVENTS[e])

    def act_y(e, middle):
        row = event_row(e, fy)
        arrived(BLK, yr.at[e])
        relay(over_x(e, True), row, 1, e, (me, fx))
        to_core(row, *EVENTS[e])

    def act_r(e, middle):
        arrived(BLK, rr.at[e])
        to_core(event_row(e, fd), *EVENTS[e])

    def act_g(n, middle):
        row = row_of(pair, core, 4 * PAIRED[1] + (fr, fx)[n])
        arrived(BLK, zr.at[N_EV + n])
        if n == 0 and middle:
            across_from_pair(PAIRED[1], row)
        send(None, row, BLK, 2, yr.at[N_EV + n], (me, fy))
        to_core(row, *PAIRED)

    def act_t(n, middle):
        arrived(BLK, yr.at[N_EV + n])
        to_core(row_of(pair, core, 4 * PAIRED[1] + (fy, fd)[n]), *PAIRED)

    def act_d(n, middle):
        row = row_of(pair, core, 4 * DIRECT[1] + (fr + n) % 4)
        arrived(BLK, zr.at[N_EV + 2 + n])
        if n == 0 and middle:
            across_from_pair(DIRECT[1], row)
        to_core(row, *DIRECT)

    actions = {
        "a": act_a, "q": act_q, "b": act_b, "s": act_s, "O": act_O, "H": act_H, "U": act_U, "F": act_F, "z": act_z,
        "x": act_x, "y": act_y, "r": act_r, "g": act_g, "t": act_t, "d": act_d,
    }
    orders = [list(END_ORDER), list(MID_ORDER)]

    def run(until):
        def steps(middle):
            order = orders[middle]
            while order and order[0] != until:
                name = order.pop(0)
                actions[name[0]](int(name[1:] or 0), middle)
            if order:
                order.pop(0)

        pl.when(mid == 0)(lambda: steps(False))
        pl.when(is_mid)(lambda: steps(True))

    run("cE")
    inputs[0].wait()
    inputs[1].wait()
    two = len_ref[0, 0] > 1
    cot_bf = cot_ref[...]
    edge_up[0] = jnp.where(two, cot_bf[PIX:], cot_bf[:PIX])
    edge_up[1] = cot_bf[:PIX]
    inputs[2].wait()
    lat_bf = lat_ref[: 2 * PIX, :]
    edge_lat[0] = jnp.where(two, lat_bf[PIX:], lat_bf[:PIX])
    edge_lat[1] = lat_bf[:PIX]
    lat_copies = halo(edge_lat, (lat_ref.at[2 * PIX : 3 * PIX], lat_ref.at[3 * PIX : 4 * PIX]), 0)
    up_copies = halo(edge_up, (halo_up.at[0], halo_up.at[1]), 2)

    def from_core(k, j):
        arrived(4 * BLK, pr.at[3 * k + j])

    def chunk_rows(p):
        return pl.ds(pl.multiple_of(TROWS + p * CHUNK, 128), CHUNK)

    def chunk_lanes(p):
        return pl.ds(pl.multiple_of(p * STRIDE, 128), CHUNK)

    def forward(p):
        acc[...] += dot32(patches[:, chunk_lanes(p)], wbuf[chunk_rows(p), :])

    def backward(p):
        grad = lax.dot_general(
            sgrad[...], wbuf[chunk_rows(p), :], NT, preferred_element_type=jnp.float32
        )
        patch_grad[:, chunk_lanes(p)] += grad

    channel = lax.broadcasted_iota(jnp.int32, (CH, 128), 0)
    group = lax.broadcasted_iota(jnp.int32, (CH, 128), 1) * (CH // GROUPS)
    gather_m = ((channel >= group) & (channel < group + CH // GROUPS)).astype(jnp.float32).astype(jnp.bfloat16)
    channel = lax.broadcasted_iota(jnp.int32, (128, CH), 1)
    group = lax.broadcasted_iota(jnp.int32, (128, CH), 0) * (CH // GROUPS)
    spread_m = ((channel >= group) & (channel < group + CH // GROUPS)).astype(jnp.float32).astype(jnp.bfloat16)
    size = PIX * (CH // GROUPS)

    column = lax.broadcasted_iota(jnp.int32, (4 * PIX, CH), 0) % WW

    def normalise():
        for copy in inputs[3:]:
            copy.wait()
        halo_arrived(lat_copies)
        values = lat_ref[...].astype(jnp.float32)
        centre = group_means(stack8(frame_sums(values)), gather_m, spread_m, size)
        centred = values - on_cells(centre[0:4])
        spread = group_means(stack8(frame_sums(centred * centred)), gather_m, spread_m, size)
        inverse = lax.rsqrt(spread + epsilon)
        inv_s[...] = inverse
        scaled = centred * on_cells(inverse[0:4])
        scaled_s[...] = scaled[: 2 * PIX]
        shifted_s[...] = scaled * gain_ref[...].reshape(1, CH) + bias_ref[...].reshape(1, CH)

    def make_patches():
        shifted = shifted_s[...]
        sigma = jax.nn.sigmoid(shifted)
        active = (shifted * sigma).astype(jnp.bfloat16).astype(jnp.float32)
        own, own_sigma = shifted[: 2 * PIX], sigma[: 2 * PIX]
        slope = own_sigma * (1.0 + own * (1.0 - own_sigma))
        slope_s[...] = slope * gain_ref[...].reshape(1, CH)
        zero = jnp.zeros((WW, CH), jnp.bfloat16)
        for dx in range(3):
            if dx == 1:
                moved = active
            elif dx == 0:
                moved = jnp.where(column == 0, 0.0, pltpu.roll(active, 1, 0))
            else:
                moved = jnp.where(column == WW - 1, 0.0, pltpu.roll(active, 4 * PIX - 1, 0))
            moved = moved.astype(jnp.bfloat16)
            quarters = [moved[q * WW : (q + 1) * WW] for q in range(8)]
            for dy in range(3):
                lanes = slice((3 * dy + dx) * CH, (3 * dy + dx + 1) * CH)
                for q in range(8):
                    if dy == 1:
                        rows = quarters[q]
                    elif dy == 0:
                        rows = quarters[q - 1] if q % 2 else zero
                    else:
                        rows = zero if q % 2 else quarters[q + 1]
                    patches[q * WW : (q + 1) * WW, lanes] = rows

    def spatial_gradient():
        halo_arrived(up_copies)
        first, second = cot_bf[:PIX], cot_bf[PIX:]
        none = jnp.zeros((PIX, CH), jnp.bfloat16)
        second = jnp.where(two, second, none)
        before_edge = halo_up[0]
        after_edge = halo_up[1]
        current = jnp.concatenate([first, second], axis=0)
        before = jnp.concatenate([before_edge, first], axis=0)
        after = jnp.concatenate([jnp.where(two, second, after_edge), after_edge], axis=0)
        grad = lax.dot_general(current, wbuf[CH : 2 * CH, :], NT, preferred_element_type=jnp.float32)
        grad += lax.dot_general(after, wbuf[0:CH, :], NT, preferred_element_type=jnp.float32)
        grad += lax.dot_general(before, wbuf[2 * CH : 3 * CH, :], NT, preferred_element_type=jnp.float32)
        sgrad[...] = grad.astype(jnp.bfloat16)

    acc[...] = jnp.zeros((4 * PIX, CH), jnp.float32)
    patch_grad[...] = jnp.zeros((2 * PIX, 9 * CH), jnp.float32)

    run("cN")
    normalise()
    run("cM")
    make_patches()
    run("cO")
    local_t.wait()
    local_s.wait()
    arrived(240, orr.at[0])
    arrived(720, orr.at[1])
    forward(plane)
    run("cS")
    from_core(A, 0)
    from_core(B, 0)
    from_core(C, 0)
    spatial_gradient()
    run("cV")
    backward(plane)
    run("cB")
    from_core(B, 1)
    from_core(B, 2)
    forward(plane_of(B))
    backward(plane_of(B))
    run("cA")
    from_core(A, 1)
    from_core(A, 2)
    forward(plane_of(A))
    backward(plane_of(A))
    run("cC")
    from_core(C, 1)
    from_core(C, 2)
    run("cT")
    last = dot32(patches[:, chunk_lanes(plane_of(C))], wbuf[chunk_rows(plane_of(C)), :])
    spat[...] = (acc[...] + last).astype(jnp.bfloat16)
    backward(plane_of(C))

    total = jnp.zeros((2 * PIX, CH), jnp.float32)
    none = jnp.zeros((WW, CH), jnp.float32)
    for dx in range(3):
        def tap(dy, q):
            k = 3 * dy + dx
            return patch_grad[q * WW : (q + 1) * WW, k * CH : (k + 1) * CH]
        parts = []
        for base in (0, 2):
            parts.append(tap(1, base) + tap(0, base + 1))
            parts.append(tap(1, base + 1) + tap(2, base))
        summed = jnp.concatenate(parts, axis=0)
        if dx == 0:
            summed = jnp.where(column[: 2 * PIX] == WW - 1, 0.0, pltpu.roll(summed, 2 * PIX - 1, 0))
        elif dx == 2:
            summed = jnp.where(column[: 2 * PIX] == 0, 0.0, pltpu.roll(summed, 1, 0))
        total = total + summed
    scaled = scaled_s[...]
    norm_grad = total * slope_s[...]
    sums = frame_sums(norm_grad) + frame_sums(norm_grad * scaled)
    means = group_means(stack8(sums), gather_m, spread_m, size)
    first = on_cells(means[0:2])
    second = on_cells(means[2:4])
    inverse = on_cells(inv_s[0:2, :])
    grad = cot_ref[...].astype(jnp.float32) + inverse * (norm_grad - first - scaled * second)
    ig_ref[:PIX, :] = grad[:PIX].astype(jnp.bfloat16)
    ig_ref[PIX:, :] = jnp.where(two, grad[PIX:], 0.0).astype(jnp.bfloat16)

    ig_copy = pltpu.make_async_copy(ig_ref, ig_any, out_sem.at[0])
    ig_copy.start()

    empty = jnp.zeros((PIX, CH), jnp.bfloat16)
    before_edge = jnp.where(fr > 0, spat[2 * PIX : 3 * PIX, :], empty)
    after_edge = jnp.where(fr < 3, spat[3 * PIX :, :], empty)
    before = jnp.concatenate([before_edge, spat[:PIX, :]], axis=0)
    after = jnp.concatenate([jnp.where(two, spat[PIX : 2 * PIX, :], after_edge), after_edge], axis=0)
    temporal = dot32(before, wbuf[0:CH, :]) + dot32(spat[: 2 * PIX, :], wbuf[CH : 2 * CH, :])
    temporal += dot32(after, wbuf[2 * CH : 3 * CH, :])
    result = lat_ref[: 2 * PIX, :].astype(jnp.float32) + temporal
    out_ref[:PIX, :] = result[:PIX].astype(jnp.bfloat16)
    out_ref[PIX:, :] = jnp.where(two, result[PIX:], 0.0).astype(jnp.bfloat16)
    out_copy = pltpu.make_async_copy(out_ref, out_any, out_sem.at[1])
    out_copy.start()
    halo_sent(lat_copies)
    halo_sent(up_copies)

    def all_sent(lane, count):
        view = wbuf.at[pl.ds(0, count)]
        pltpu.make_async_remote_copy(
            src_ref=view, dst_ref=view, send_sem=sent.at[lane], recv_sem=orr.at[0],
            device_id=(other, fr), device_id_type=MESH,
        ).wait_send()

    all_sent(0, 7 * BLK)
    pl.when(is_mid)(lambda: all_sent(0, 12 * BLK))
    for n, here in ((0, jnp.logical_not(centre_column)), (1, centre_column)):
        turned = len(OVER_X[n])
        pl.when(here)(lambda turned=turned: all_sent(1, (N_EV + turned) * BLK))
        pl.when(here)(lambda turned=turned: all_sent(2, (2 * N_EV + 2 - turned) * BLK))
    all_sent(3, 48 * BLK)
    ig_copy.wait()
    out_copy.wait()


def fused(latents, lengths, norm_gain, norm_bias, spatial_weight, temporal_weight, cotangent):
    rows = 2 * PIX
    dma = pltpu.SemaphoreType.DMA
    cells = jax.ShapeDtypeStruct((rows, CH), jnp.bfloat16)
    out, grad = pl.pallas_call(
        kernel,
        out_shape=(cells, cells),
        in_specs=[pl.BlockSpec(memory_space=pltpu.MemorySpace.HBM)] * 7,
        out_specs=(pl.BlockSpec(memory_space=pl.ANY), pl.BlockSpec(memory_space=pl.ANY)),
        scratch_shapes=[
            pltpu.SMEM((1, 1), jnp.int32),
            pltpu.VMEM((2 * rows, CH), jnp.bfloat16),
            pltpu.VMEM((rows, CH), jnp.bfloat16),
            pltpu.VMEM((CH,), jnp.float32),
            pltpu.VMEM((CH,), jnp.float32),
            dma((5,)),
            pltpu.VMEM((TROWS + PLANES * CHUNK, CH), jnp.bfloat16),
            pltpu.VMEM((2 * rows, 9 * CH), jnp.bfloat16),
            pltpu.VMEM((rows, 9 * CH), jnp.float32),
            pltpu.VMEM((2 * rows, CH), jnp.float32),
            pltpu.VMEM((rows, CH), jnp.bfloat16),
            pltpu.VMEM((rows, CH), jnp.float32),
            pltpu.VMEM((2 * rows, CH), jnp.float32),
            pltpu.VMEM((8, CH), jnp.float32),
            pltpu.VMEM((rows, CH), jnp.float32),
            pltpu.VMEM((2 * rows, CH), jnp.bfloat16),
            pltpu.VMEM((rows, CH), jnp.bfloat16),
            pltpu.VMEM((rows, CH), jnp.bfloat16),
            dma((2,)),
        ] + [pltpu.VMEM((2, PIX, CH), jnp.bfloat16)] * 3
        + [dma((n,)) for n in (2, 4, N_EV + 6, N_EV, N_EV + 2, N_EV, 9, 2, 4, 4)],
        compiler_params=pltpu.CompilerParams(
            collective_id=0, has_side_effects=True, vmem_limit_bytes=107 << 19
        ),
    )(
        lengths, latents.reshape(rows, CH), cotangent.reshape(rows, CH),
        norm_gain, norm_bias, spatial_weight, temporal_weight,
    )
    return (out.reshape(latents.shape), grad.reshape(latents.shape))


def solution(mesh):
    in_specs = (
        P("dp", "frames", None, None, None),
        P("dp", "frames"),
        P(),
        P(),
        P("dp", None),
        P("dp", None),
        P("dp", "frames", None, None, None),
    )
    out_specs = (P("dp", "frames", None, None, None), P("dp", "frames", None, None, None))
    small = mesh.shape["dp"] == 2 * PLANES and mesh.shape["frames"] == 4
    body = fused if small else shards
    return jax.shard_map(body, mesh=mesh, in_specs=in_specs, out_specs=out_specs, check_vma=False)
```

```python
import functools

import jax
import jax.numpy as jnp
from jax import lax
from jax.experimental import pallas as pl
from jax.experimental.pallas import tpu as pltpu
from jax.sharding import PartitionSpec as P

CH = 640
GROUPS = 32
HH = 2
WW = 32
PIX = 64


epsilon = 1e-05


def padded_2(cells, sides, width):
    for axis, dim in sides:
        count = lax.axis_size(axis)
        ends = count - 1
        head = lax.slice_in_dim(cells, 0, width, axis=dim)
        tail = lax.slice_in_dim(cells, cells.shape[dim] - width, cells.shape[dim], axis=dim)
        cells = jnp.concatenate(
            [
                lax.ppermute(tail, axis, [(i, (i + 1) % count) for i in range(ends)]),
                cells,
                lax.ppermute(head, axis, [((i + 1) % count, i) for i in range(ends)]),
            ],
            axis=dim,
        )
    return cells


def normalize(frames_in, norm_gain, norm_bias):
    shaped = frames_in.reshape(frames_in.shape[0], -1, GROUPS, CH // GROUPS)
    centre = jnp.mean(shaped, axis=(1, 3), keepdims=True)
    spread = jnp.mean(jnp.square(shaped - centre), axis=(1, 3), keepdims=True)
    inverse = lax.rsqrt(spread + epsilon)
    scaled = (shaped - centre) * inverse
    shifted = scaled.reshape(frames_in.shape) * norm_gain + norm_bias
    return (scaled, inverse, shifted)


def norm_backward(active_grad, scaled, inverse, shifted, norm_gain):
    sigma = jax.nn.sigmoid(shifted)
    shift_grad = active_grad * sigma * (1.0 + shifted * (1.0 - sigma))
    norm_grad = (shift_grad * norm_gain).reshape(scaled.shape)
    first = jnp.mean(norm_grad, axis=(1, 3), keepdims=True)
    second = jnp.mean(norm_grad * scaled, axis=(1, 3), keepdims=True)
    return (inverse * (norm_grad - first - scaled * second)).reshape(active_grad.shape)


def patchify(active):
    padded = jnp.pad(active, ((0, 0), (1, 1), (1, 1), (0, 0)))
    pieces = [padded[:, row : row + HH, col : col + WW, :] for row in range(3) for col in range(3)]
    return jnp.concatenate(pieces, axis=-1).reshape(-1, 9 * CH)


def unpatchify(patch_grad):
    count = patch_grad.shape[0] // (HH * WW)
    shaped = patch_grad.reshape(count, HH, WW, 9, CH)
    total = jnp.zeros((count, HH + 2, WW + 2, CH), jnp.float32)
    for row in range(3):
        for col in range(3):
            total = total + jnp.pad(
                shaped[:, :, :, row * 3 + col, :], ((0, 0), (row, 2 - row), (col, 2 - col), (0, 0))
            )
    return total[:, 1:-1, 1:-1, :]


def contract_rows(left, right):
    return lax.dot_general(
        left, right, (((1,), (1,)), ((), ())), preferred_element_type=jnp.float32
    )


def neighbours(frames_bf, count):
    last_frame = lax.dynamic_index_in_dim(frames_bf, count - 1, 0, keepdims=False)
    boundary = jnp.stack([frames_bf[0], last_frame])
    padded = padded_2(boundary, (("frames", 0),), 1)
    before_frames = jnp.concatenate([padded[0:1], frames_bf[:-1]])
    candidate = jnp.concatenate([frames_bf[1:], padded[3:4]])
    places = jnp.arange(frames_bf.shape[0], dtype=jnp.int32)
    after_frames = jnp.where((places + 1 < count)[:, None, None], candidate, padded[3:4])
    return (before_frames, after_frames)


def shards(latents, lengths, norm_gain, norm_bias, spatial_weight, temporal_weight, cotangent):
    clip_in = latents[0]
    clip_cot = cotangent[0]
    slots_here = clip_in.shape[0]
    count = lengths[0, 0]
    valid = jnp.arange(slots_here, dtype=jnp.int32) < count
    keep = valid[:, None, None, None]
    spatial_full, temporal_full = (
        lax.all_gather(spatial_weight, "dp", axis=0, tiled=True),
        lax.all_gather(temporal_weight, "dp", axis=0, tiled=True),
    )
    first_w = temporal_full[:CH]
    centre_w = temporal_full[CH : 2 * CH]
    last_w = temporal_full[2 * CH :]
    values = clip_in.astype(jnp.float32)
    scaled, inverse, shifted = normalize(values, norm_gain, norm_bias)
    active = jax.nn.silu(shifted).astype(jnp.bfloat16)
    patches = patchify(active)
    spatial = jnp.dot(patches, spatial_full, preferred_element_type=jnp.float32)
    spatial = spatial.astype(jnp.bfloat16).reshape(slots_here, PIX, CH)
    earlier, later_frames = neighbours(spatial, count)
    temporal = jnp.dot(earlier.reshape(-1, CH), first_w, preferred_element_type=jnp.float32)
    temporal = temporal + jnp.dot(
        spatial.reshape(-1, CH), centre_w, preferred_element_type=jnp.float32
    )
    temporal = temporal + jnp.dot(
        later_frames.reshape(-1, CH), last_w, preferred_element_type=jnp.float32
    )
    temporal = temporal.reshape(slots_here, HH, WW, CH)
    output = jnp.where(keep, values + temporal, 0.0).astype(jnp.bfloat16)
    upstream = jnp.where(keep, clip_cot, jnp.zeros_like(clip_cot)).reshape(slots_here, PIX, CH)
    up_before, up_after = neighbours(upstream, count)
    spatial_grad = contract_rows(upstream.reshape(-1, CH), centre_w)
    spatial_grad = spatial_grad + contract_rows(up_after.reshape(-1, CH), first_w)
    spatial_grad = spatial_grad + contract_rows(up_before.reshape(-1, CH), last_w)
    spatial_grad = spatial_grad.astype(jnp.bfloat16)
    patch_grad = contract_rows(spatial_grad, spatial_full)
    active_grad = unpatchify(patch_grad)
    latent_grad = norm_backward(active_grad, scaled, inverse, shifted, norm_gain)
    input_grad = jnp.where(keep, clip_cot.astype(jnp.float32) + latent_grad, 0.0).astype(
        jnp.bfloat16
    )
    return (output[None], input_grad[None])

MESH = pl.DeviceIdType.MESH
BLK = 80
PLANES = 4
TROWS = 3 * CH
CHUNK = 1536
STRIDE = 1408
A, B, C = range(3)
EVENTS = ((A, 0), (B, 0), (C, 0), (B, 1), (B, 2), (C, 1), (C, 2))
PAIRED = (A, 1)
DIRECT = (A, 2)
N_EV = len(EVENTS)
OVER_X = ((0, 1, 4, 5), (0, 1, 4, 5))
END_ORDER = (
    "a", "cE", "U", "b", "z0", "g0", "s", "H", "g1", "y0", "z1", "cN", "z2", "z3", "cM", "z4", "r0",
    "y1", "x0", "O", "x1", "x2", "cO", "x3", "z5", "z6", "y4", "r2", "r1", "y2", "cS", "x4", "cV",
    "y3", "x6", "t0", "x5", "y5", "r3", "r4", "y6", "d2", "d0", "d3", "d1", "t1", "cB", "r6", "r5",
    "cA", "cC", "cT",
)
MID_ORDER = (
    "a", "cE", "q", "b", "H", "F0", "z0", "F1", "g0", "z1", "F2", "z2", "F3", "y0", "d0", "z3",
    "d1", "F4", "y1", "cN", "x0", "z4", "cM", "F5", "x2", "g1", "U", "O", "F6", "cO", "s", "x1",
    "z5", "x3", "d2", "t0", "z6", "y4", "r0", "r1", "r2", "y3", "y2", "cS", "x4", "d3", "t1", "x5",
    "y5", "x6", "cV", "r3", "r4", "y6", "cB", "r5", "r6", "cA", "cC", "cT",
)
NT = (((1,), (1,)), ((), ()))


def row_of(plane, core, block):
    late = (block + 9) // 12
    early_row = (2 * plane + core) * 240 + block * BLK
    late_row = TROWS + plane * (CHUNK + 32) + core * 720 + (block - 3) * BLK
    return pl.multiple_of((1 - late) * early_row + late * late_row, 16)


def split3(rows):
    high = rows.astype(jnp.bfloat16)
    rest = rows - high.astype(jnp.float32)
    mid = rest.astype(jnp.bfloat16)
    low = (rest - mid.astype(jnp.float32)).astype(jnp.bfloat16)
    return high, mid, low


def dot32(left, right):
    return jnp.dot(left, right, preferred_element_type=jnp.float32)


def group_means(rows, gather_m, spread_m, size):
    high, mid, low = split3(rows)
    sums = dot32(high, gather_m) + dot32(mid, gather_m) + dot32(low, gather_m)
    high, mid, low = split3(sums * (1.0 / size))
    return dot32(high, spread_m) + dot32(mid, spread_m) + dot32(low, spread_m)


def frame_sums(cells):
    return tuple(
        jnp.sum(cells[at : at + PIX], axis=0, keepdims=True) for at in range(0, cells.shape[0], PIX)
    )


def stack8(rows):
    return jnp.concatenate(list(rows) + [jnp.zeros((8 - len(rows), CH), jnp.float32)], axis=0)


def on_cells(rows):
    return jnp.concatenate(
        [jnp.broadcast_to(rows[n : n + 1], (PIX, CH)) for n in range(rows.shape[0])], axis=0
    )


def kernel(
    len_hbm, lat_hbm, cot_hbm, gain_hbm, bias_hbm, ws_ref, wt_ref,
    out_any, ig_any,
    len_ref, lat_ref, cot_ref, gain_ref, bias_ref, in_sem, wbuf, patches, patch_grad, acc, sgrad, scaled_s, shifted_s, inv_s, slope_s, spat, out_ref, ig_ref, out_sem, edge_up, edge_lat, halo_up,
    own_sem, sent, zr, xr, yr, rr, pr, orr, hs, hr,
):
    me = lax.axis_index("dp")
    fr = lax.axis_index("frames")
    plane = me // 2
    core = me % 2
    other = me + 1 - 2 * core
    fx = fr + 1 - 2 * (fr % 2)
    fy = (fr + 2) % 4
    fd = 3 - fr
    right = (fr + 1) % 4
    left = (fr + 3) % 4

    mid = (plane + 1) // 2 % 2
    is_mid = mid == 1
    pair = plane + 1 - 2 * (plane % 2)
    inner = 2 - plane // 2
    outer = 3 - 3 * (plane // 2)
    across = 3 - plane

    def plane_of(slot):
        return (pair, inner, outer)[slot]

    barrier = pltpu.get_barrier_semaphore()
    pl.semaphore_signal(barrier, inc=1, device_id=(2 * pair + core, fr), device_id_type=MESH)

    @pl.when(is_mid)
    def _():
        pl.semaphore_signal(barrier, inc=1, device_id=(2 * across + core, fr), device_id_type=MESH)

    for f in (fx, fy):
        pl.semaphore_signal(barrier, inc=1, device_id=(me, f), device_id_type=MESH)
    centre = (fr + 1) // 2 % 2

    @pl.when(centre == 1)
    def _():
        pl.semaphore_signal(barrier, inc=1, device_id=(me, fd), device_id_type=MESH)

    pl.semaphore_signal(barrier, inc=1, device_id=(other, fr), device_id_type=MESH)

    own_t = pl.multiple_of(me * 240, 16)
    own_s = pl.multiple_of(TROWS + plane * (CHUNK + 32) + core * 720, 16)
    inputs = [
        pltpu.make_async_copy(src, dst, in_sem.at[n])
        for n, (src, dst) in enumerate(
            ((len_hbm, len_ref), (cot_hbm, cot_ref), (lat_hbm, lat_ref.at[0 : 2 * PIX]), (gain_hbm, gain_ref), (bias_hbm, bias_ref))
        )
    ]
    for copy in inputs:
        copy.start()
    local_t = pltpu.make_async_copy(wt_ref, wbuf.at[pl.ds(own_t, 240)], own_sem.at[0])
    local_s = pltpu.make_async_copy(ws_ref, wbuf.at[pl.ds(own_s, 720)], own_sem.at[1])
    local_t.start()
    local_s.start()

    for p in range(PLANES):
        base = TROWS + p * CHUNK
        if p > 0:
            wbuf[base : base + 32 * p, :] = jnp.zeros((32 * p, CH), jnp.bfloat16)
        if p < 3:
            wbuf[base + 1440 + 32 * p : base + CHUNK, :] = jnp.zeros((96 - 32 * p, CH), jnp.bfloat16)

    @pl.when(fr == 0)
    def _():
        lat_ref[2 * PIX : 3 * PIX, :] = jnp.zeros((PIX, CH), jnp.bfloat16)
        halo_up[0] = jnp.zeros((PIX, CH), jnp.bfloat16)

    @pl.when(fr == 3)
    def _():
        lat_ref[3 * PIX :, :] = jnp.zeros((PIX, CH), jnp.bfloat16)
        halo_up[1] = jnp.zeros((PIX, CH), jnp.bfloat16)

    pl.semaphore_wait(barrier, 4 + mid + centre)

    def send(src, row, count, lane, recv_sem, device):
        view = wbuf.at[pl.ds(row, count)]
        pltpu.make_async_remote_copy(
            src_ref=view if src is None else src, dst_ref=view, send_sem=sent.at[lane], recv_sem=recv_sem,
            device_id=device, device_id_type=MESH,
        ).start()

    def arrived(count, recv_sem):
        view = wbuf.at[pl.ds(0, count)]
        pltpu.make_async_remote_copy(
            src_ref=view, dst_ref=view, send_sem=sent.at[0], recv_sem=recv_sem,
            device_id=(other, fr), device_id_type=MESH,
        ).wait_recv()

    def halo(edge, dest, k):
        return [
            pltpu.make_async_remote_copy(
                src_ref=edge.at[side], dst_ref=dest[side], send_sem=hs.at[k + side],
                recv_sem=hr.at[k + side], device_id=(me, device), device_id_type=MESH,
            )
            for side, device in ((0, right), (1, left))
        ]

    def halo_start(copies):
        pl.when(fr < 3)(copies[0].start)
        pl.when(fr > 0)(copies[1].start)

    def halo_arrived(copies):
        pl.when(fr > 0)(copies[0].wait_recv)
        pl.when(fr < 3)(copies[1].wait_recv)

    def halo_sent(copies):
        pl.when(fr < 3)(copies[0].wait_send)
        pl.when(fr > 0)(copies[1].wait_send)

    def z_send(p, view, src, recv_sem):
        pltpu.make_async_remote_copy(
            src_ref=src, dst_ref=view, send_sem=sent.at[0], recv_sem=recv_sem,
            device_id=(2 * p + core, fr), device_id_type=MESH,
        ).start()

    def z_sem(slot, j):
        return zr.at[EVENTS.index((slot, j))]

    def z_own(p, j, f, recv_sem):
        view = wbuf.at[pl.ds(row_of(plane, core, 4 * j + f), BLK)]
        if j > 0:
            at = pl.multiple_of((4 * j + f - 3) * BLK, 16)
            z_send(p, view, ws_ref.at[pl.ds(at, BLK)], recv_sem)
            return

        @pl.when(f < 3)
        def _():
            z_send(p, view, wt_ref.at[pl.ds(pl.multiple_of((f % 3) * BLK, 16), BLK)], recv_sem)

        @pl.when(f == 3)
        def _():
            z_send(p, view, ws_ref.at[pl.ds(0, BLK)], recv_sem)

    def across_from_pair(j, row):
        view = wbuf.at[pl.ds(row, BLK)]
        z_send(across, view, view, z_sem(C, j))
        if j < 2:
            z_own(across, j + 1, fr, z_sem(B, j + 1))

    def to_core(row, k, j):
        send(None, row, BLK, 3, pr.at[3 * k + j], (other, fr))

    def event_row(e, f):
        k, j = EVENTS[e]
        return row_of(plane_of(k), core, 4 * j + f)

    centre_column = centre == 1

    def over_x(e, value):
        routes = [(e in OVER_X[n]) == value for n in range(2)]
        if routes[0] == routes[1]:
            return routes[0]
        return centre_column if routes[1] else jnp.logical_not(centre_column)

    def relay(condition, row, lane, e, device):
        def go():
            send(None, row, BLK, lane, rr.at[e], device)

        if condition is True:
            go()
        elif condition is not False:
            pl.when(condition)(go)

    def act_a(n, middle):
        z_own(pair, 0, fr, z_sem(A, 0))

    def act_q(n, middle):
        z_own(across, 0, fr, z_sem(B, 0))

    def act_b(n, middle):
        for g, f in enumerate((fr, fx)):
            z_own(pair, 1, f, zr.at[N_EV + g])

    def act_s(n, middle):
        for d in range(4):
            z_own(pair, 2, (fr + d) % 4, zr.at[N_EV + 2 + d])

    def act_O(n, middle):
        send(wt_ref, own_t, 240, 3, orr.at[0], (other, fr))
        send(ws_ref, own_s, 720, 3, orr.at[1], (other, fr))

    def act_H(n, middle):
        halo_start(lat_copies)

    def act_U(n, middle):
        halo_start(up_copies)

    def act_F(e, middle):
        k, j = EVENTS[e]
        row = event_row(e, fr)
        arrived(BLK, zr.at[e])
        if k == A:
            across_from_pair(j, row)
        else:
            z_send(pair, wbuf.at[pl.ds(row, BLK)], wbuf.at[pl.ds(row, BLK)], z_sem(k, j))

    def act_z(e, middle):
        row = event_row(e, fr)
        if not middle:
            arrived(BLK, zr.at[e])
        send(None, row, BLK, 1, xr.at[e], (me, fx))
        send(None, row, BLK, 2, yr.at[e], (me, fy))
        to_core(row, *EVENTS[e])

    def act_x(e, middle):
        row = event_row(e, fx)
        arrived(BLK, xr.at[e])
        relay(over_x(e, False), row, 2, e, (me, fy))
        to_core(row, *EVENTS[e])

    def act_y(e, middle):
        row = event_row(e, fy)
        arrived(BLK, yr.at[e])
        relay(over_x(e, True), row, 1, e, (me, fx))
        to_core(row, *EVENTS[e])

    def act_r(e, middle):
        arrived(BLK, rr.at[e])
        to_core(event_row(e, fd), *EVENTS[e])

    def act_g(n, middle):
        row = row_of(pair, core, 4 * PAIRED[1] + (fr, fx)[n])
        arrived(BLK, zr.at[N_EV + n])
        if n == 0 and middle:
            across_from_pair(PAIRED[1], row)
        send(None, row, BLK, 2, yr.at[N_EV + n], (me, fy))
        to_core(row, *PAIRED)

    def act_t(n, middle):
        arrived(BLK, yr.at[N_EV + n])
        to_core(row_of(pair, core, 4 * PAIRED[1] + (fy, fd)[n]), *PAIRED)

    def act_d(n, middle):
        row = row_of(pair, core, 4 * DIRECT[1] + (fr + n) % 4)
        arrived(BLK, zr.at[N_EV + 2 + n])
        if n == 0 and middle:
            across_from_pair(DIRECT[1], row)
        to_core(row, *DIRECT)

    actions = {
        "a": act_a, "q": act_q, "b": act_b, "s": act_s, "O": act_O, "H": act_H, "U": act_U, "F": act_F, "z": act_z,
        "x": act_x, "y": act_y, "r": act_r, "g": act_g, "t": act_t, "d": act_d,
    }
    orders = [list(END_ORDER), list(MID_ORDER)]

    def run(until):
        def steps(middle):
            order = orders[middle]
            while order and order[0] != until:
                name = order.pop(0)
                actions[name[0]](int(name[1:] or 0), middle)
            if order:
                order.pop(0)

        pl.when(mid == 0)(lambda: steps(False))
        pl.when(is_mid)(lambda: steps(True))

    run("cE")
    inputs[0].wait()
    inputs[1].wait()
    two = len_ref[0, 0] > 1
    cot_bf = cot_ref[...]
    edge_up[0] = jnp.where(two, cot_bf[PIX:], cot_bf[:PIX])
    edge_up[1] = cot_bf[:PIX]
    inputs[2].wait()
    lat_bf = lat_ref[: 2 * PIX, :]
    edge_lat[0] = jnp.where(two, lat_bf[PIX:], lat_bf[:PIX])
    edge_lat[1] = lat_bf[:PIX]
    lat_copies = halo(edge_lat, (lat_ref.at[2 * PIX : 3 * PIX], lat_ref.at[3 * PIX : 4 * PIX]), 0)
    up_copies = halo(edge_up, (halo_up.at[0], halo_up.at[1]), 2)

    def from_core(k, j):
        arrived(4 * BLK, pr.at[3 * k + j])

    def chunk_rows(p):
        return pl.ds(pl.multiple_of(TROWS + p * CHUNK, 128), CHUNK)

    def chunk_lanes(p):
        return pl.ds(pl.multiple_of(p * STRIDE, 128), CHUNK)

    def forward(p):
        acc[...] += dot32(patches[:, chunk_lanes(p)], wbuf[chunk_rows(p), :])

    def backward(p):
        grad = lax.dot_general(
            sgrad[...], wbuf[chunk_rows(p), :], NT, preferred_element_type=jnp.float32
        )
        patch_grad[:, chunk_lanes(p)] += grad

    channel = lax.broadcasted_iota(jnp.int32, (CH, 128), 0)
    group = lax.broadcasted_iota(jnp.int32, (CH, 128), 1) * (CH // GROUPS)
    gather_m = ((channel >= group) & (channel < group + CH // GROUPS)).astype(jnp.float32).astype(jnp.bfloat16)
    channel = lax.broadcasted_iota(jnp.int32, (128, CH), 1)
    group = lax.broadcasted_iota(jnp.int32, (128, CH), 0) * (CH // GROUPS)
    spread_m = ((channel >= group) & (channel < group + CH // GROUPS)).astype(jnp.float32).astype(jnp.bfloat16)
    size = PIX * (CH // GROUPS)

    column = lax.broadcasted_iota(jnp.int32, (4 * PIX, CH), 0) % WW

    def normalise():
        for copy in inputs[3:]:
            copy.wait()
        halo_arrived(lat_copies)
        values = lat_ref[...].astype(jnp.float32)
        centre = group_means(stack8(frame_sums(values)), gather_m, spread_m, size)
        centred = values - on_cells(centre[0:4])
        spread = group_means(stack8(frame_sums(centred * centred)), gather_m, spread_m, size)
        inverse = lax.rsqrt(spread + epsilon)
        inv_s[...] = inverse
        scaled = centred * on_cells(inverse[0:4])
        scaled_s[...] = scaled[: 2 * PIX]
        shifted_s[...] = scaled * gain_ref[...].reshape(1, CH) + bias_ref[...].reshape(1, CH)

    def make_patches():
        shifted = shifted_s[...]
        sigma = jax.nn.sigmoid(shifted)
        active = (shifted * sigma).astype(jnp.bfloat16).astype(jnp.float32)
        own, own_sigma = shifted[: 2 * PIX], sigma[: 2 * PIX]
        slope = own_sigma * (1.0 + own * (1.0 - own_sigma))
        slope_s[...] = slope * gain_ref[...].reshape(1, CH)
        zero = jnp.zeros((WW, CH), jnp.bfloat16)
        for dx in range(3):
            if dx == 1:
                moved = active
            elif dx == 0:
                moved = jnp.where(column == 0, 0.0, pltpu.roll(active, 1, 0))
            else:
                moved = jnp.where(column == WW - 1, 0.0, pltpu.roll(active, 4 * PIX - 1, 0))
            moved = moved.astype(jnp.bfloat16)
            quarters = [moved[q * WW : (q + 1) * WW] for q in range(8)]
            for dy in range(3):
                lanes = slice((3 * dy + dx) * CH, (3 * dy + dx + 1) * CH)
                for q in range(8):
                    if dy == 1:
                        rows = quarters[q]
                    elif dy == 0:
                        rows = quarters[q - 1] if q % 2 else zero
                    else:
                        rows = zero if q % 2 else quarters[q + 1]
                    patches[q * WW : (q + 1) * WW, lanes] = rows

    def spatial_gradient():
        halo_arrived(up_copies)
        first, second = cot_bf[:PIX], cot_bf[PIX:]
        none = jnp.zeros((PIX, CH), jnp.bfloat16)
        second = jnp.where(two, second, none)
        before_edge = halo_up[0]
        after_edge = halo_up[1]
        current = jnp.concatenate([first, second], axis=0)
        before = jnp.concatenate([before_edge, first], axis=0)
        after = jnp.concatenate([jnp.where(two, second, after_edge), after_edge], axis=0)
        grad = lax.dot_general(current, wbuf[CH : 2 * CH, :], NT, preferred_element_type=jnp.float32)
        grad += lax.dot_general(after, wbuf[0:CH, :], NT, preferred_element_type=jnp.float32)
        grad += lax.dot_general(before, wbuf[2 * CH : 3 * CH, :], NT, preferred_element_type=jnp.float32)
        sgrad[...] = grad.astype(jnp.bfloat16)

    acc[...] = jnp.zeros((4 * PIX, CH), jnp.float32)
    patch_grad[...] = jnp.zeros((2 * PIX, 9 * CH), jnp.float32)

    run("cN")
    normalise()
    run("cM")
    make_patches()
    run("cO")
    local_t.wait()
    local_s.wait()
    arrived(240, orr.at[0])
    arrived(720, orr.at[1])
    forward(plane)
    run("cS")
    from_core(A, 0)
    from_core(B, 0)
    from_core(C, 0)
    spatial_gradient()
    run("cV")
    backward(plane)
    run("cB")
    from_core(B, 1)
    from_core(B, 2)
    forward(plane_of(B))
    backward(plane_of(B))
    run("cA")
    from_core(A, 1)
    from_core(A, 2)
    forward(plane_of(A))
    backward(plane_of(A))
    run("cC")
    from_core(C, 1)
    from_core(C, 2)
    run("cT")
    last = dot32(patches[:, chunk_lanes(plane_of(C))], wbuf[chunk_rows(plane_of(C)), :])
    spat[...] = (acc[...] + last).astype(jnp.bfloat16)
    backward(plane_of(C))

    empty = jnp.zeros((PIX, CH), jnp.bfloat16)
    before_edge = jnp.where(fr > 0, spat[2 * PIX : 3 * PIX, :], empty)
    after_edge = jnp.where(fr < 3, spat[3 * PIX :, :], empty)
    before = jnp.concatenate([before_edge, spat[:PIX, :]], axis=0)
    after = jnp.concatenate([jnp.where(two, spat[PIX : 2 * PIX, :], after_edge), after_edge], axis=0)
    temporal = dot32(before, wbuf[0:CH, :]) + dot32(spat[: 2 * PIX, :], wbuf[CH : 2 * CH, :])
    temporal += dot32(after, wbuf[2 * CH : 3 * CH, :])
    result = lat_ref[: 2 * PIX, :].astype(jnp.float32) + temporal
    out_ref[:PIX, :] = result[:PIX].astype(jnp.bfloat16)
    out_ref[PIX:, :] = jnp.where(two, result[PIX:], 0.0).astype(jnp.bfloat16)
    total = jnp.zeros((2 * PIX, CH), jnp.float32)
    none = jnp.zeros((WW, CH), jnp.float32)
    for dx in range(3):
        def tap(dy, q):
            k = 3 * dy + dx
            return patch_grad[q * WW : (q + 1) * WW, k * CH : (k + 1) * CH]
        parts = []
        for base in (0, 2):
            parts.append(tap(1, base) + tap(0, base + 1))
            parts.append(tap(1, base + 1) + tap(2, base))
        summed = jnp.concatenate(parts, axis=0)
        if dx == 0:
            summed = jnp.where(column[: 2 * PIX] == WW - 1, 0.0, pltpu.roll(summed, 2 * PIX - 1, 0))
        elif dx == 2:
            summed = jnp.where(column[: 2 * PIX] == 0, 0.0, pltpu.roll(summed, 1, 0))
        total = total + summed
    scaled = scaled_s[...]
    norm_grad = total * slope_s[...]
    sums = frame_sums(norm_grad) + frame_sums(norm_grad * scaled)
    means = group_means(stack8(sums), gather_m, spread_m, size)
    first = on_cells(means[0:2])
    second = on_cells(means[2:4])
    inverse = on_cells(inv_s[0:2, :])
    grad = cot_ref[...].astype(jnp.float32) + inverse * (norm_grad - first - scaled * second)
    ig_ref[:PIX, :] = grad[:PIX].astype(jnp.bfloat16)
    ig_ref[PIX:, :] = jnp.where(two, grad[PIX:], 0.0).astype(jnp.bfloat16)

    out_copy = pltpu.make_async_copy(out_ref, out_any, out_sem.at[1])
    out_copy.start()
    ig_copy = pltpu.make_async_copy(ig_ref, ig_any, out_sem.at[0])
    ig_copy.start()
    halo_sent(lat_copies)
    halo_sent(up_copies)

    def all_sent(lane, count):
        view = wbuf.at[pl.ds(0, count)]
        pltpu.make_async_remote_copy(
            src_ref=view, dst_ref=view, send_sem=sent.at[lane], recv_sem=orr.at[0],
            device_id=(other, fr), device_id_type=MESH,
        ).wait_send()

    all_sent(0, 7 * BLK)
    pl.when(is_mid)(lambda: all_sent(0, 12 * BLK))
    for n, here in ((0, jnp.logical_not(centre_column)), (1, centre_column)):
        turned = len(OVER_X[n])
        pl.when(here)(lambda turned=turned: all_sent(1, (N_EV + turned) * BLK))
        pl.when(here)(lambda turned=turned: all_sent(2, (2 * N_EV + 2 - turned) * BLK))
    all_sent(3, 48 * BLK)
    ig_copy.wait()
    out_copy.wait()


def fused(latents, lengths, norm_gain, norm_bias, spatial_weight, temporal_weight, cotangent):
    rows = 2 * PIX
    dma = pltpu.SemaphoreType.DMA
    cells = jax.ShapeDtypeStruct((rows, CH), jnp.bfloat16)
    out, grad = pl.pallas_call(
        kernel,
        out_shape=(cells, cells),
        in_specs=[pl.BlockSpec(memory_space=pltpu.MemorySpace.HBM)] * 7,
        out_specs=(pl.BlockSpec(memory_space=pl.ANY), pl.BlockSpec(memory_space=pl.ANY)),
        scratch_shapes=[
            pltpu.SMEM((1, 1), jnp.int32),
            pltpu.VMEM((2 * rows, CH), jnp.bfloat16),
            pltpu.VMEM((rows, CH), jnp.bfloat16),
            pltpu.VMEM((CH,), jnp.float32),
            pltpu.VMEM((CH,), jnp.float32),
            dma((5,)),
            pltpu.VMEM((TROWS + PLANES * CHUNK, CH), jnp.bfloat16),
            pltpu.VMEM((2 * rows, 9 * CH), jnp.bfloat16),
            pltpu.VMEM((rows, 9 * CH), jnp.float32),
            pltpu.VMEM((2 * rows, CH), jnp.float32),
            pltpu.VMEM((rows, CH), jnp.bfloat16),
            pltpu.VMEM((rows, CH), jnp.float32),
            pltpu.VMEM((2 * rows, CH), jnp.float32),
            pltpu.VMEM((8, CH), jnp.float32),
            pltpu.VMEM((rows, CH), jnp.float32),
            pltpu.VMEM((2 * rows, CH), jnp.bfloat16),
            pltpu.VMEM((rows, CH), jnp.bfloat16),
            pltpu.VMEM((rows, CH), jnp.bfloat16),
            dma((2,)),
        ] + [pltpu.VMEM((2, PIX, CH), jnp.bfloat16)] * 3
        + [dma((n,)) for n in (2, 4, N_EV + 6, N_EV, N_EV + 2, N_EV, 9, 2, 4, 4)],
        compiler_params=pltpu.CompilerParams(
            collective_id=0, has_side_effects=True, vmem_limit_bytes=107 << 19
        ),
    )(
        lengths, latents.reshape(rows, CH), cotangent.reshape(rows, CH),
        norm_gain, norm_bias, spatial_weight, temporal_weight,
    )
    return (out.reshape(latents.shape), grad.reshape(latents.shape))


def solution(mesh):
    in_specs = (
        P("dp", "frames", None, None, None),
        P("dp", "frames"),
        P(),
        P(),
        P("dp", None),
        P("dp", None),
        P("dp", "frames", None, None, None),
    )
    out_specs = (P("dp", "frames", None, None, None), P("dp", "frames", None, None, None))
    small = mesh.shape["dp"] == 2 * PLANES and mesh.shape["frames"] == 4
    body = fused if small else shards
    return jax.shard_map(body, mesh=mesh, in_specs=in_specs, out_specs=out_specs, check_vma=False)
```

```python
import functools

import jax
import jax.numpy as jnp
from jax import lax
from jax.experimental import pallas as pl
from jax.experimental.pallas import tpu as pltpu
from jax.sharding import PartitionSpec as P

CH = 640
GROUPS = 32
HH = 2
WW = 32
PIX = 64


epsilon = 1e-05


def padded_2(cells, sides, width):
    for axis, dim in sides:
        count = lax.axis_size(axis)
        ends = count - 1
        head = lax.slice_in_dim(cells, 0, width, axis=dim)
        tail = lax.slice_in_dim(cells, cells.shape[dim] - width, cells.shape[dim], axis=dim)
        cells = jnp.concatenate(
            [
                lax.ppermute(tail, axis, [(i, (i + 1) % count) for i in range(ends)]),
                cells,
                lax.ppermute(head, axis, [((i + 1) % count, i) for i in range(ends)]),
            ],
            axis=dim,
        )
    return cells


def normalize(frames_in, norm_gain, norm_bias):
    shaped = frames_in.reshape(frames_in.shape[0], -1, GROUPS, CH // GROUPS)
    centre = jnp.mean(shaped, axis=(1, 3), keepdims=True)
    spread = jnp.mean(jnp.square(shaped - centre), axis=(1, 3), keepdims=True)
    inverse = lax.rsqrt(spread + epsilon)
    scaled = (shaped - centre) * inverse
    shifted = scaled.reshape(frames_in.shape) * norm_gain + norm_bias
    return (scaled, inverse, shifted)


def norm_backward(active_grad, scaled, inverse, shifted, norm_gain):
    sigma = jax.nn.sigmoid(shifted)
    shift_grad = active_grad * sigma * (1.0 + shifted * (1.0 - sigma))
    norm_grad = (shift_grad * norm_gain).reshape(scaled.shape)
    first = jnp.mean(norm_grad, axis=(1, 3), keepdims=True)
    second = jnp.mean(norm_grad * scaled, axis=(1, 3), keepdims=True)
    return (inverse * (norm_grad - first - scaled * second)).reshape(active_grad.shape)


def patchify(active):
    padded = jnp.pad(active, ((0, 0), (1, 1), (1, 1), (0, 0)))
    pieces = [padded[:, row : row + HH, col : col + WW, :] for row in range(3) for col in range(3)]
    return jnp.concatenate(pieces, axis=-1).reshape(-1, 9 * CH)


def unpatchify(patch_grad):
    count = patch_grad.shape[0] // (HH * WW)
    shaped = patch_grad.reshape(count, HH, WW, 9, CH)
    total = jnp.zeros((count, HH + 2, WW + 2, CH), jnp.float32)
    for row in range(3):
        for col in range(3):
            total = total + jnp.pad(
                shaped[:, :, :, row * 3 + col, :], ((0, 0), (row, 2 - row), (col, 2 - col), (0, 0))
            )
    return total[:, 1:-1, 1:-1, :]


def contract_rows(left, right):
    return lax.dot_general(
        left, right, (((1,), (1,)), ((), ())), preferred_element_type=jnp.float32
    )


def neighbours(frames_bf, count):
    last_frame = lax.dynamic_index_in_dim(frames_bf, count - 1, 0, keepdims=False)
    boundary = jnp.stack([frames_bf[0], last_frame])
    padded = padded_2(boundary, (("frames", 0),), 1)
    before_frames = jnp.concatenate([padded[0:1], frames_bf[:-1]])
    candidate = jnp.concatenate([frames_bf[1:], padded[3:4]])
    places = jnp.arange(frames_bf.shape[0], dtype=jnp.int32)
    after_frames = jnp.where((places + 1 < count)[:, None, None], candidate, padded[3:4])
    return (before_frames, after_frames)


def shards(latents, lengths, norm_gain, norm_bias, spatial_weight, temporal_weight, cotangent):
    clip_in = latents[0]
    clip_cot = cotangent[0]
    slots_here = clip_in.shape[0]
    count = lengths[0, 0]
    valid = jnp.arange(slots_here, dtype=jnp.int32) < count
    keep = valid[:, None, None, None]
    spatial_full, temporal_full = (
        lax.all_gather(spatial_weight, "dp", axis=0, tiled=True),
        lax.all_gather(temporal_weight, "dp", axis=0, tiled=True),
    )
    first_w = temporal_full[:CH]
    centre_w = temporal_full[CH : 2 * CH]
    last_w = temporal_full[2 * CH :]
    values = clip_in.astype(jnp.float32)
    scaled, inverse, shifted = normalize(values, norm_gain, norm_bias)
    active = jax.nn.silu(shifted).astype(jnp.bfloat16)
    patches = patchify(active)
    spatial = jnp.dot(patches, spatial_full, preferred_element_type=jnp.float32)
    spatial = spatial.astype(jnp.bfloat16).reshape(slots_here, PIX, CH)
    earlier, later_frames = neighbours(spatial, count)
    temporal = jnp.dot(earlier.reshape(-1, CH), first_w, preferred_element_type=jnp.float32)
    temporal = temporal + jnp.dot(
        spatial.reshape(-1, CH), centre_w, preferred_element_type=jnp.float32
    )
    temporal = temporal + jnp.dot(
        later_frames.reshape(-1, CH), last_w, preferred_element_type=jnp.float32
    )
    temporal = temporal.reshape(slots_here, HH, WW, CH)
    output = jnp.where(keep, values + temporal, 0.0).astype(jnp.bfloat16)
    upstream = jnp.where(keep, clip_cot, jnp.zeros_like(clip_cot)).reshape(slots_here, PIX, CH)
    up_before, up_after = neighbours(upstream, count)
    spatial_grad = contract_rows(upstream.reshape(-1, CH), centre_w)
    spatial_grad = spatial_grad + contract_rows(up_after.reshape(-1, CH), first_w)
    spatial_grad = spatial_grad + contract_rows(up_before.reshape(-1, CH), last_w)
    spatial_grad = spatial_grad.astype(jnp.bfloat16)
    patch_grad = contract_rows(spatial_grad, spatial_full)
    active_grad = unpatchify(patch_grad)
    latent_grad = norm_backward(active_grad, scaled, inverse, shifted, norm_gain)
    input_grad = jnp.where(keep, clip_cot.astype(jnp.float32) + latent_grad, 0.0).astype(
        jnp.bfloat16
    )
    return (output[None], input_grad[None])

MESH = pl.DeviceIdType.MESH
BLK = 80
PLANES = 4
TROWS = 3 * CH
CHUNK = 1536
STRIDE = 1408
A, B, C = range(3)
EVENTS = ((A, 0), (B, 0), (C, 0), (B, 1), (B, 2), (C, 1), (C, 2))
PAIRED = (A, 1)
DIRECT = (A, 2)
N_EV = len(EVENTS)
OVER_X = ((0, 1, 4, 5), (0, 1, 4, 5))
END_ORDER = (
    "a", "cE", "U", "b", "z0", "g0", "s", "H", "g1", "y0", "z1", "cN", "z2", "z3", "cM", "z4", "r0",
    "y1", "x0", "O", "x1", "x2", "cO", "x3", "z5", "z6", "y4", "r2", "r1", "y2", "cS", "x4", "cV",
    "y3", "x6", "t0", "x5", "y5", "r3", "r4", "y6", "d2", "d0", "d3", "d1", "t1", "cB", "r6", "r5",
    "cA", "cC", "cT",
)
MID_ORDER = (
    "a", "cE", "q", "b", "H", "F0", "z0", "F1", "g0", "z1", "F2", "z2", "F3", "y0", "d0", "z3",
    "d1", "F4", "y1", "cN", "x0", "z4", "cM", "F5", "x2", "g1", "U", "O", "F6", "cO", "s", "x1",
    "z5", "x3", "d2", "t0", "z6", "y4", "r0", "r1", "r2", "y3", "y2", "cS", "x4", "d3", "t1", "x5",
    "y5", "x6", "cV", "r3", "r4", "y6", "cB", "r5", "r6", "cA", "cC", "cT",
)
NT = (((1,), (1,)), ((), ()))


def row_of(plane, core, block):
    late = (block + 9) // 12
    early_row = (2 * plane + core) * 240 + block * BLK
    late_row = TROWS + plane * (CHUNK + 32) + core * 720 + (block - 3) * BLK
    return pl.multiple_of((1 - late) * early_row + late * late_row, 16)


def split3(rows):
    high = rows.astype(jnp.bfloat16)
    rest = rows - high.astype(jnp.float32)
    mid = rest.astype(jnp.bfloat16)
    low = (rest - mid.astype(jnp.float32)).astype(jnp.bfloat16)
    return high, mid, low


def dot32(left, right):
    return jnp.dot(left, right, preferred_element_type=jnp.float32)


def group_means(rows, gather_m, spread_m, size):
    high, mid, low = split3(rows)
    sums = dot32(high, gather_m) + dot32(mid, gather_m) + dot32(low, gather_m)
    high, mid, low = split3(sums * (1.0 / size))
    return dot32(high, spread_m) + dot32(mid, spread_m) + dot32(low, spread_m)


def frame_sums(cells):
    return tuple(
        jnp.sum(cells[at : at + PIX], axis=0, keepdims=True) for at in range(0, cells.shape[0], PIX)
    )


def stack8(rows):
    return jnp.concatenate(list(rows) + [jnp.zeros((8 - len(rows), CH), jnp.float32)], axis=0)


def on_cells(rows):
    return jnp.concatenate(
        [jnp.broadcast_to(rows[n : n + 1], (PIX, CH)) for n in range(rows.shape[0])], axis=0
    )


def kernel(
    len_hbm, lat_hbm, cot_hbm, gain_hbm, bias_hbm, ws_ref, wt_ref,
    out_any, ig_any,
    len_ref, lat_ref, cot_ref, gain_ref, bias_ref, in_sem, wbuf, patches, patch_grad, acc, sgrad, scaled_s, shifted_s, inv_s, slope_s, spat, out_ref, ig_ref, out_sem, edge_up, edge_lat, halo_up,
    own_sem, sent, zr, xr, yr, rr, pr, orr, hs, hr,
):
    me = lax.axis_index("dp")
    fr = lax.axis_index("frames")
    plane = me // 2
    core = me % 2
    other = me + 1 - 2 * core
    fx = fr + 1 - 2 * (fr % 2)
    fy = (fr + 2) % 4
    fd = 3 - fr
    right = (fr + 1) % 4
    left = (fr + 3) % 4

    mid = (plane + 1) // 2 % 2
    is_mid = mid == 1
    pair = plane + 1 - 2 * (plane % 2)
    inner = 2 - plane // 2
    outer = 3 - 3 * (plane // 2)
    across = 3 - plane

    def plane_of(slot):
        return (pair, inner, outer)[slot]

    barrier = pltpu.get_barrier_semaphore()
    pl.semaphore_signal(barrier, inc=1, device_id=(2 * pair + core, fr), device_id_type=MESH)

    @pl.when(is_mid)
    def _():
        pl.semaphore_signal(barrier, inc=1, device_id=(2 * across + core, fr), device_id_type=MESH)

    for f in (fx, fy):
        pl.semaphore_signal(barrier, inc=1, device_id=(me, f), device_id_type=MESH)
    centre = (fr + 1) // 2 % 2

    @pl.when(centre == 1)
    def _():
        pl.semaphore_signal(barrier, inc=1, device_id=(me, fd), device_id_type=MESH)

    pl.semaphore_signal(barrier, inc=1, device_id=(other, fr), device_id_type=MESH)

    own_t = pl.multiple_of(me * 240, 16)
    own_s = pl.multiple_of(TROWS + plane * (CHUNK + 32) + core * 720, 16)
    inputs = [
        pltpu.make_async_copy(src, dst, in_sem.at[n])
        for n, (src, dst) in enumerate(
            ((len_hbm, len_ref), (cot_hbm, cot_ref), (lat_hbm, lat_ref.at[0 : 2 * PIX]), (gain_hbm, gain_ref), (bias_hbm, bias_ref))
        )
    ]
    for copy in inputs:
        copy.start()
    local_t = pltpu.make_async_copy(wt_ref, wbuf.at[pl.ds(own_t, 240)], own_sem.at[0])
    local_s = pltpu.make_async_copy(ws_ref, wbuf.at[pl.ds(own_s, 720)], own_sem.at[1])
    local_t.start()
    local_s.start()

    for p in range(PLANES):
        base = TROWS + p * CHUNK
        if p > 0:
            wbuf[base : base + 32 * p, :] = jnp.zeros((32 * p, CH), jnp.bfloat16)
        if p < 3:
            wbuf[base + 1440 + 32 * p : base + CHUNK, :] = jnp.zeros((96 - 32 * p, CH), jnp.bfloat16)

    @pl.when(fr == 0)
    def _():
        lat_ref[2 * PIX : 3 * PIX, :] = jnp.zeros((PIX, CH), jnp.bfloat16)
        halo_up[0] = jnp.zeros((PIX, CH), jnp.bfloat16)

    @pl.when(fr == 3)
    def _():
        lat_ref[3 * PIX :, :] = jnp.zeros((PIX, CH), jnp.bfloat16)
        halo_up[1] = jnp.zeros((PIX, CH), jnp.bfloat16)

    acc[...] = jnp.zeros((4 * PIX, CH), jnp.float32)
    patch_grad[...] = jnp.zeros((2 * PIX, 9 * CH), jnp.float32)
    inputs[0].wait()
    inputs[1].wait()
    two = len_ref[0, 0] > 1
    cot_bf = cot_ref[...]
    edge_up[0] = jnp.where(two, cot_bf[PIX:], cot_bf[:PIX])
    edge_up[1] = cot_bf[:PIX]
    inputs[2].wait()
    lat_bf = lat_ref[: 2 * PIX, :]
    edge_lat[0] = jnp.where(two, lat_bf[PIX:], lat_bf[:PIX])
    edge_lat[1] = lat_bf[:PIX]

    pl.semaphore_wait(barrier, 4 + mid + centre)

    def send(src, row, count, lane, recv_sem, device):
        view = wbuf.at[pl.ds(row, count)]
        pltpu.make_async_remote_copy(
            src_ref=view if src is None else src, dst_ref=view, send_sem=sent.at[lane], recv_sem=recv_sem,
            device_id=device, device_id_type=MESH,
        ).start()

    def arrived(count, recv_sem):
        view = wbuf.at[pl.ds(0, count)]
        pltpu.make_async_remote_copy(
            src_ref=view, dst_ref=view, send_sem=sent.at[0], recv_sem=recv_sem,
            device_id=(other, fr), device_id_type=MESH,
        ).wait_recv()

    def halo(edge, dest, k):
        return [
            pltpu.make_async_remote_copy(
                src_ref=edge.at[side], dst_ref=dest[side], send_sem=hs.at[k + side],
                recv_sem=hr.at[k + side], device_id=(me, device), device_id_type=MESH,
            )
            for side, device in ((0, right), (1, left))
        ]

    def halo_start(copies):
        pl.when(fr < 3)(copies[0].start)
        pl.when(fr > 0)(copies[1].start)

    def halo_arrived(copies):
        pl.when(fr > 0)(copies[0].wait_recv)
        pl.when(fr < 3)(copies[1].wait_recv)

    def halo_sent(copies):
        pl.when(fr < 3)(copies[0].wait_send)
        pl.when(fr > 0)(copies[1].wait_send)

    def z_send(p, view, src, recv_sem):
        pltpu.make_async_remote_copy(
            src_ref=src, dst_ref=view, send_sem=sent.at[0], recv_sem=recv_sem,
            device_id=(2 * p + core, fr), device_id_type=MESH,
        ).start()

    def z_sem(slot, j):
        return zr.at[EVENTS.index((slot, j))]

    def z_own(p, j, f, recv_sem):
        view = wbuf.at[pl.ds(row_of(plane, core, 4 * j + f), BLK)]
        if j > 0:
            at = pl.multiple_of((4 * j + f - 3) * BLK, 16)
            z_send(p, view, ws_ref.at[pl.ds(at, BLK)], recv_sem)
            return

        @pl.when(f < 3)
        def _():
            z_send(p, view, wt_ref.at[pl.ds(pl.multiple_of((f % 3) * BLK, 16), BLK)], recv_sem)

        @pl.when(f == 3)
        def _():
            z_send(p, view, ws_ref.at[pl.ds(0, BLK)], recv_sem)

    def across_from_pair(j, row):
        view = wbuf.at[pl.ds(row, BLK)]
        z_send(across, view, view, z_sem(C, j))
        if j < 2:
            z_own(across, j + 1, fr, z_sem(B, j + 1))

    def to_core(row, k, j):
        send(None, row, BLK, 3, pr.at[3 * k + j], (other, fr))

    def event_row(e, f):
        k, j = EVENTS[e]
        return row_of(plane_of(k), core, 4 * j + f)

    centre_column = centre == 1

    def over_x(e, value):
        routes = [(e in OVER_X[n]) == value for n in range(2)]
        if routes[0] == routes[1]:
            return routes[0]
        return centre_column if routes[1] else jnp.logical_not(centre_column)

    def relay(condition, row, lane, e, device):
        def go():
            send(None, row, BLK, lane, rr.at[e], device)

        if condition is True:
            go()
        elif condition is not False:
            pl.when(condition)(go)

    def act_a(n, middle):
        z_own(pair, 0, fr, z_sem(A, 0))

    def act_q(n, middle):
        z_own(across, 0, fr, z_sem(B, 0))

    def act_b(n, middle):
        for g, f in enumerate((fr, fx)):
            z_own(pair, 1, f, zr.at[N_EV + g])

    def act_s(n, middle):
        for d in range(4):
            z_own(pair, 2, (fr + d) % 4, zr.at[N_EV + 2 + d])

    def act_O(n, middle):
        send(wt_ref, own_t, 240, 3, orr.at[0], (other, fr))
        send(ws_ref, own_s, 720, 3, orr.at[1], (other, fr))

    def act_H(n, middle):
        halo_start(lat_copies)

    def act_U(n, middle):
        halo_start(up_copies)

    def act_F(e, middle):
        k, j = EVENTS[e]
        row = event_row(e, fr)
        arrived(BLK, zr.at[e])
        if k == A:
            across_from_pair(j, row)
        else:
            z_send(pair, wbuf.at[pl.ds(row, BLK)], wbuf.at[pl.ds(row, BLK)], z_sem(k, j))

    def act_z(e, middle):
        row = event_row(e, fr)
        if not middle:
            arrived(BLK, zr.at[e])
        send(None, row, BLK, 1, xr.at[e], (me, fx))
        send(None, row, BLK, 2, yr.at[e], (me, fy))
        to_core(row, *EVENTS[e])

    def act_x(e, middle):
        row = event_row(e, fx)
        arrived(BLK, xr.at[e])
        relay(over_x(e, False), row, 2, e, (me, fy))
        to_core(row, *EVENTS[e])

    def act_y(e, middle):
        row = event_row(e, fy)
        arrived(BLK, yr.at[e])
        relay(over_x(e, True), row, 1, e, (me, fx))
        to_core(row, *EVENTS[e])

    def act_r(e, middle):
        arrived(BLK, rr.at[e])
        to_core(event_row(e, fd), *EVENTS[e])

    def act_g(n, middle):
        row = row_of(pair, core, 4 * PAIRED[1] + (fr, fx)[n])
        arrived(BLK, zr.at[N_EV + n])
        if n == 0 and middle:
            across_from_pair(PAIRED[1], row)
        send(None, row, BLK, 2, yr.at[N_EV + n], (me, fy))
        to_core(row, *PAIRED)

    def act_t(n, middle):
        arrived(BLK, yr.at[N_EV + n])
        to_core(row_of(pair, core, 4 * PAIRED[1] + (fy, fd)[n]), *PAIRED)

    def act_d(n, middle):
        row = row_of(pair, core, 4 * DIRECT[1] + (fr + n) % 4)
        arrived(BLK, zr.at[N_EV + 2 + n])
        if n == 0 and middle:
            across_from_pair(DIRECT[1], row)
        to_core(row, *DIRECT)

    actions = {
        "a": act_a, "q": act_q, "b": act_b, "s": act_s, "O": act_O, "H": act_H, "U": act_U, "F": act_F, "z": act_z,
        "x": act_x, "y": act_y, "r": act_r, "g": act_g, "t": act_t, "d": act_d,
    }
    orders = [list(END_ORDER), list(MID_ORDER)]

    def run(until):
        def steps(middle):
            order = orders[middle]
            while order and order[0] != until:
                name = order.pop(0)
                actions[name[0]](int(name[1:] or 0), middle)
            if order:
                order.pop(0)

        pl.when(mid == 0)(lambda: steps(False))
        pl.when(is_mid)(lambda: steps(True))

    run("cE")
    lat_copies = halo(edge_lat, (lat_ref.at[2 * PIX : 3 * PIX], lat_ref.at[3 * PIX : 4 * PIX]), 0)
    up_copies = halo(edge_up, (halo_up.at[0], halo_up.at[1]), 2)

    def from_core(k, j):
        arrived(4 * BLK, pr.at[3 * k + j])

    def chunk_rows(p):
        return pl.ds(pl.multiple_of(TROWS + p * CHUNK, 128), CHUNK)

    def chunk_lanes(p):
        return pl.ds(pl.multiple_of(p * STRIDE, 128), CHUNK)

    def forward(p):
        acc[...] += dot32(patches[:, chunk_lanes(p)], wbuf[chunk_rows(p), :])

    def backward(p):
        grad = lax.dot_general(
            sgrad[...], wbuf[chunk_rows(p), :], NT, preferred_element_type=jnp.float32
        )
        patch_grad[:, chunk_lanes(p)] += grad

    channel = lax.broadcasted_iota(jnp.int32, (CH, 128), 0)
    group = lax.broadcasted_iota(jnp.int32, (CH, 128), 1) * (CH // GROUPS)
    gather_m = ((channel >= group) & (channel < group + CH // GROUPS)).astype(jnp.float32).astype(jnp.bfloat16)
    channel = lax.broadcasted_iota(jnp.int32, (128, CH), 1)
    group = lax.broadcasted_iota(jnp.int32, (128, CH), 0) * (CH // GROUPS)
    spread_m = ((channel >= group) & (channel < group + CH // GROUPS)).astype(jnp.float32).astype(jnp.bfloat16)
    size = PIX * (CH // GROUPS)

    column = lax.broadcasted_iota(jnp.int32, (4 * PIX, CH), 0) % WW

    def normalise():
        for copy in inputs[3:]:
            copy.wait()
        halo_arrived(lat_copies)
        values = lat_ref[...].astype(jnp.float32)
        centre = group_means(stack8(frame_sums(values)), gather_m, spread_m, size)
        centred = values - on_cells(centre[0:4])
        spread = group_means(stack8(frame_sums(centred * centred)), gather_m, spread_m, size)
        inverse = lax.rsqrt(spread + epsilon)
        inv_s[...] = inverse
        scaled = centred * on_cells(inverse[0:4])
        scaled_s[...] = scaled[: 2 * PIX]
        shifted_s[...] = scaled * gain_ref[...].reshape(1, CH) + bias_ref[...].reshape(1, CH)

    def make_patches():
        shifted = shifted_s[...]
        sigma = jax.nn.sigmoid(shifted)
        active = (shifted * sigma).astype(jnp.bfloat16).astype(jnp.float32)
        own, own_sigma = shifted[: 2 * PIX], sigma[: 2 * PIX]
        slope = own_sigma * (1.0 + own * (1.0 - own_sigma))
        slope_s[...] = slope * gain_ref[...].reshape(1, CH)
        zero = jnp.zeros((WW, CH), jnp.bfloat16)
        for dx in range(3):
            if dx == 1:
                moved = active
            elif dx == 0:
                moved = jnp.where(column == 0, 0.0, pltpu.roll(active, 1, 0))
            else:
                moved = jnp.where(column == WW - 1, 0.0, pltpu.roll(active, 4 * PIX - 1, 0))
            moved = moved.astype(jnp.bfloat16)
            quarters = [moved[q * WW : (q + 1) * WW] for q in range(8)]
            for dy in range(3):
                lanes = slice((3 * dy + dx) * CH, (3 * dy + dx + 1) * CH)
                for q in range(8):
                    if dy == 1:
                        rows = quarters[q]
                    elif dy == 0:
                        rows = quarters[q - 1] if q % 2 else zero
                    else:
                        rows = zero if q % 2 else quarters[q + 1]
                    patches[q * WW : (q + 1) * WW, lanes] = rows

    def spatial_gradient():
        halo_arrived(up_copies)
        first, second = cot_bf[:PIX], cot_bf[PIX:]
        none = jnp.zeros((PIX, CH), jnp.bfloat16)
        second = jnp.where(two, second, none)
        before_edge = halo_up[0]
        after_edge = halo_up[1]
        current = jnp.concatenate([first, second], axis=0)
        before = jnp.concatenate([before_edge, first], axis=0)
        after = jnp.concatenate([jnp.where(two, second, after_edge), after_edge], axis=0)
        grad = lax.dot_general(current, wbuf[CH : 2 * CH, :], NT, preferred_element_type=jnp.float32)
        grad += lax.dot_general(after, wbuf[0:CH, :], NT, preferred_element_type=jnp.float32)
        grad += lax.dot_general(before, wbuf[2 * CH : 3 * CH, :], NT, preferred_element_type=jnp.float32)
        sgrad[...] = grad.astype(jnp.bfloat16)


    run("cN")
    normalise()
    run("cM")
    make_patches()
    run("cO")
    local_t.wait()
    local_s.wait()
    arrived(240, orr.at[0])
    arrived(720, orr.at[1])
    forward(plane)
    run("cS")
    from_core(A, 0)
    from_core(B, 0)
    from_core(C, 0)
    spatial_gradient()
    run("cV")
    backward(plane)
    run("cB")
    from_core(B, 1)
    from_core(B, 2)
    forward(plane_of(B))
    backward(plane_of(B))
    run("cA")
    from_core(A, 1)
    from_core(A, 2)
    forward(plane_of(A))
    backward(plane_of(A))
    run("cC")
    from_core(C, 1)
    from_core(C, 2)
    run("cT")
    last = dot32(patches[:, chunk_lanes(plane_of(C))], wbuf[chunk_rows(plane_of(C)), :])
    spat[...] = (acc[...] + last).astype(jnp.bfloat16)
    backward(plane_of(C))

    empty = jnp.zeros((PIX, CH), jnp.bfloat16)
    before_edge = jnp.where(fr > 0, spat[2 * PIX : 3 * PIX, :], empty)
    after_edge = jnp.where(fr < 3, spat[3 * PIX :, :], empty)
    before = jnp.concatenate([before_edge, spat[:PIX, :]], axis=0)
    after = jnp.concatenate([jnp.where(two, spat[PIX : 2 * PIX, :], after_edge), after_edge], axis=0)
    temporal = dot32(before, wbuf[0:CH, :]) + dot32(spat[: 2 * PIX, :], wbuf[CH : 2 * CH, :])
    temporal += dot32(after, wbuf[2 * CH : 3 * CH, :])
    result = lat_ref[: 2 * PIX, :].astype(jnp.float32) + temporal
    out_ref[:PIX, :] = result[:PIX].astype(jnp.bfloat16)
    out_ref[PIX:, :] = jnp.where(two, result[PIX:], 0.0).astype(jnp.bfloat16)
    total = jnp.zeros((2 * PIX, CH), jnp.float32)
    none = jnp.zeros((WW, CH), jnp.float32)
    for dx in range(3):
        def tap(dy, q):
            k = 3 * dy + dx
            return patch_grad[q * WW : (q + 1) * WW, k * CH : (k + 1) * CH]
        parts = []
        for base in (0, 2):
            parts.append(tap(1, base) + tap(0, base + 1))
            parts.append(tap(1, base + 1) + tap(2, base))
        summed = jnp.concatenate(parts, axis=0)
        if dx == 0:
            summed = jnp.where(column[: 2 * PIX] == WW - 1, 0.0, pltpu.roll(summed, 2 * PIX - 1, 0))
        elif dx == 2:
            summed = jnp.where(column[: 2 * PIX] == 0, 0.0, pltpu.roll(summed, 1, 0))
        total = total + summed
    scaled = scaled_s[...]
    norm_grad = total * slope_s[...]
    sums = frame_sums(norm_grad) + frame_sums(norm_grad * scaled)
    means = group_means(stack8(sums), gather_m, spread_m, size)
    first = on_cells(means[0:2])
    second = on_cells(means[2:4])
    inverse = on_cells(inv_s[0:2, :])
    grad = cot_ref[...].astype(jnp.float32) + inverse * (norm_grad - first - scaled * second)
    ig_ref[:PIX, :] = grad[:PIX].astype(jnp.bfloat16)
    ig_ref[PIX:, :] = jnp.where(two, grad[PIX:], 0.0).astype(jnp.bfloat16)

    out_copy = pltpu.make_async_copy(out_ref, out_any, out_sem.at[1])
    out_copy.start()
    ig_copy = pltpu.make_async_copy(ig_ref, ig_any, out_sem.at[0])
    ig_copy.start()
    halo_sent(lat_copies)
    halo_sent(up_copies)

    def all_sent(lane, count):
        view = wbuf.at[pl.ds(0, count)]
        pltpu.make_async_remote_copy(
            src_ref=view, dst_ref=view, send_sem=sent.at[lane], recv_sem=orr.at[0],
            device_id=(other, fr), device_id_type=MESH,
        ).wait_send()

    all_sent(0, 7 * BLK)
    pl.when(is_mid)(lambda: all_sent(0, 12 * BLK))
    for n, here in ((0, jnp.logical_not(centre_column)), (1, centre_column)):
        turned = len(OVER_X[n])
        pl.when(here)(lambda turned=turned: all_sent(1, (N_EV + turned) * BLK))
        pl.when(here)(lambda turned=turned: all_sent(2, (2 * N_EV + 2 - turned) * BLK))
    all_sent(3, 48 * BLK)
    ig_copy.wait()
    out_copy.wait()


def fused(latents, lengths, norm_gain, norm_bias, spatial_weight, temporal_weight, cotangent):
    rows = 2 * PIX
    dma = pltpu.SemaphoreType.DMA
    cells = jax.ShapeDtypeStruct((rows, CH), jnp.bfloat16)
    out, grad = pl.pallas_call(
        kernel,
        out_shape=(cells, cells),
        in_specs=[pl.BlockSpec(memory_space=pltpu.MemorySpace.HBM)] * 7,
        out_specs=(pl.BlockSpec(memory_space=pl.ANY), pl.BlockSpec(memory_space=pl.ANY)),
        scratch_shapes=[
            pltpu.SMEM((1, 1), jnp.int32),
            pltpu.VMEM((2 * rows, CH), jnp.bfloat16),
            pltpu.VMEM((rows, CH), jnp.bfloat16),
            pltpu.VMEM((CH,), jnp.float32),
            pltpu.VMEM((CH,), jnp.float32),
            dma((5,)),
            pltpu.VMEM((TROWS + PLANES * CHUNK, CH), jnp.bfloat16),
            pltpu.VMEM((2 * rows, 9 * CH), jnp.bfloat16),
            pltpu.VMEM((rows, 9 * CH), jnp.float32),
            pltpu.VMEM((2 * rows, CH), jnp.float32),
            pltpu.VMEM((rows, CH), jnp.bfloat16),
            pltpu.VMEM((rows, CH), jnp.float32),
            pltpu.VMEM((2 * rows, CH), jnp.float32),
            pltpu.VMEM((8, CH), jnp.float32),
            pltpu.VMEM((rows, CH), jnp.float32),
            pltpu.VMEM((2 * rows, CH), jnp.bfloat16),
            pltpu.VMEM((rows, CH), jnp.bfloat16),
            pltpu.VMEM((rows, CH), jnp.bfloat16),
            dma((2,)),
        ] + [pltpu.VMEM((2, PIX, CH), jnp.bfloat16)] * 3
        + [dma((n,)) for n in (2, 4, N_EV + 6, N_EV, N_EV + 2, N_EV, 9, 2, 4, 4)],
        compiler_params=pltpu.CompilerParams(
            collective_id=0, has_side_effects=True, vmem_limit_bytes=107 << 19
        ),
    )(
        lengths, latents.reshape(rows, CH), cotangent.reshape(rows, CH),
        norm_gain, norm_bias, spatial_weight, temporal_weight,
    )
    return (out.reshape(latents.shape), grad.reshape(latents.shape))


def solution(mesh):
    in_specs = (
        P("dp", "frames", None, None, None),
        P("dp", "frames"),
        P(),
        P(),
        P("dp", None),
        P("dp", None),
        P("dp", "frames", None, None, None),
    )
    out_specs = (P("dp", "frames", None, None, None), P("dp", "frames", None, None, None))
    small = mesh.shape["dp"] == 2 * PLANES and mesh.shape["frames"] == 4
    body = fused if small else shards
    return jax.shard_map(body, mesh=mesh, in_specs=in_specs, out_specs=out_specs, check_vma=False)
```
